512 devices in a mesh: cells: 128 (over y, z, core), samp: 4 (over x).
Axes of the slice: x: 4, y: 8, z: 8, core: 2. Of those that a mesh axis runs over, the one named last changes fastest.
Arguments:
- snapshots: bfloat16 [262144, 4096], P('cells', 'samp'), may hold values from -24 to 24
- left_slow: bfloat16 [120, 4096], P(None, 'cells'), may hold values from -0.09375 to 0.09375
- left_fast: bfloat16 [120, 64], replicated, may hold values from -0.75 to 0.75
- right_slow: bfloat16 [150, 128], P(None, 'samp'), may hold values from -0.5 to 0.5
- right_fast: bfloat16 [150, 32], replicated, may hold values from -1 to 1
Outputs:
- range_sketch: float32 [262144, 150], P(('cells', 'samp'))
- core: float32 [150, 4096], P(None, ('samp', 'cells'))
The draws below stay inside these ranges and needn't reach their ends.
All inputs are finite; a program needn't handle non-finite values.
Results may differ from the reference program's by a relative error of at most 0.012.
The reference program's roundings to bfloat16 on the way (of `psi` and `omega`) count: a program that leaves them out, or rounds other values in their place, can miss the bound.
Values sent between devices are 32-bit elements; how exact they have to be, the bound alone decides.
A program may use at most 64 MiB of HBM per device.

```python
import jax
import jax.numpy as jnp
from jax import lax

R_L = 120
R_R = 150
CB = 64
SB = 32
CA = 4096
SA = 128
CELLS = 262144
SAMPLES = 4096


def raised(array, rng, source, target, blocks, factor):
    owner, partner = [(jnp.arange(array.shape[dim]) // (array.shape[dim] // blocks)).reshape([-1 if axis == dim else 1 for axis in range(array.ndim)]) for dim in (source, target)]
    chosen = jax.random.permutation(rng, blocks)[partner]
    strong = (owner == chosen) | (owner == (partner + blocks // 2) % blocks)
    return jnp.where(strong, factor * array, array)


def shard_levels(own_key, extent, pieces, least, largest):
    def one(axis_at, blocks):
        steps = jax.random.uniform(jax.random.fold_in(jax.random.fold_in(own_key, 6), axis_at), (blocks,), jnp.float32, least / len(pieces), largest / len(pieces))
        return jnp.repeat(jnp.exp(steps), extent[axis_at] // blocks).reshape((-1,) + (1,) * (len(extent) - axis_at - 1))

    gain = one(*pieces[0])
    for cut in pieces[1:]:
        gain = gain * one(*cut)
    return gain


def noise(rng, shape, scale, limit, shards=(), held_as=jnp.bfloat16):
    gain = shard_levels(rng, shape, shards, -0.22, 0.18) if shards else 1.0
    entries = jax.random.normal(rng, shape, jnp.float32) * scale * gain
    return jnp.minimum(jnp.maximum(entries, -limit), limit).astype(held_as)


def gaussian_with(rng, extent, deviation, reach, shards, heavy, held_as=jnp.bfloat16):
    values = deviation * jax.random.normal(rng, extent, jnp.float32)
    if shards:
        values = values * shard_levels(rng, extent, shards, -0.22, 0.18)
    return jnp.clip(raised(values, jax.random.fold_in(rng, 3), *heavy), -reach, reach).astype(held_as)


def setup_inputs(seed: int = 0) -> dict:
    splits = jax.random.split(jax.random.key(seed), 6)
    snapshots = gaussian_with(splits[0], (CELLS, SAMPLES), 1.0, 24.0, ((0, 128), (1, 4)), (0, 1, 128, 5.5))
    left_slow = noise(splits[1], (R_L, CA), CA ** -0.5, 0.09375, ((1, 128),))
    left_fast = noise(splits[2], (R_L, CB), CB ** -0.5, 0.75)
    right_slow = noise(splits[3], (R_R, SA), SA ** -0.5, 0.5, ((1, 4),))
    right_fast = noise(splits[4], (R_R, SB), SB ** -0.5, 1.0)
    return dict(snapshots=snapshots, left_slow=left_slow, left_fast=left_fast, right_slow=right_slow, right_fast=right_fast)


def reference(snapshots, left_slow, left_fast, right_slow, right_fast):
    psi = (left_slow.astype(jnp.float32)[:, :, None] * left_fast.astype(jnp.float32)[:, None, :]).reshape(R_L, CA * CB).astype(jnp.bfloat16)
    omega = (right_slow.astype(jnp.float32)[:, :, None] * right_fast.astype(jnp.float32)[:, None, :]).reshape(R_R, SA * SB).astype(jnp.bfloat16)
    left_sketch = jnp.dot(psi.astype(jnp.float32), snapshots.astype(jnp.float32), preferred_element_type=jnp.float32)
    range_sketch = lax.dot_general(snapshots.astype(jnp.float32), omega.astype(jnp.float32), (((1,), (1,)), ((), ())), preferred_element_type=jnp.float32)
    core_input = jnp.dot(left_sketch, omega.astype(jnp.float32).T, precision=lax.Precision.HIGHEST)
    gram = jnp.dot(core_input, core_input.T, precision=lax.Precision.HIGHEST) + 0.5 * jnp.eye(R_L, dtype=jnp.float32)
    factor = jnp.linalg.cholesky(gram)
    solved = jax.scipy.linalg.cho_solve((factor, True), left_sketch)
    core = jnp.dot(core_input.T, solved, precision=lax.Precision.HIGHEST)
    return (range_sketch, core)
```

```python
import functools

import jax
import jax.numpy as jnp
from jax import lax
from jax.experimental import pallas as pl
from jax.experimental.pallas import tpu as pltpu
from jax.sharding import PartitionSpec as P

F32 = jnp.float32
BF16 = jnp.bfloat16
MESH = pl.DeviceIdType.MESH
NY, NZ = 8, 8
LP, RP = 128, 256
HIGHEST = lax.Precision.HIGHEST


def dot(a, b, dims, precision=None):
    return lax.dot_general(a, b, (dims, ((), ())), precision=precision, preferred_element_type=F32)


def expand_rows(slow_t, fast_t, width, start):
    ns, nf = slow_t.shape[0], fast_t.shape[0]
    n = lax.broadcasted_iota(jnp.int32, (ns, width), 1) + start
    a = lax.broadcasted_iota(jnp.int32, (ns, width), 0)
    pick_slow = jnp.where(n // nf == a, 1.0, 0.0).astype(BF16)
    n = lax.broadcasted_iota(jnp.int32, (nf, width), 1) + start
    b = lax.broadcasted_iota(jnp.int32, (nf, width), 0)
    pick_fast = jnp.where(n % nf == b, 1.0, 0.0).astype(BF16)
    dims = ((0,), (0,))
    return (dot(slow_t, pick_slow, dims) * dot(fast_t, pick_fast, dims)).astype(BF16)


def compute_kernel(x_ref, ls_ref, lf_ref, rs_ref, rf_ref, rt_ref, lt_ref, cp_ref, omega, acc):
    step = pl.program_id(0)
    rows, samples = x_ref.shape
    rank_l = ls_ref.shape[1]
    rank_r = rs_ref.shape[1]

    @pl.when(step == 0)
    def _():
        omega[...] = expand_rows(rs_ref[...], rf_ref[...], samples, 0)
        acc[...] = jnp.zeros_like(acc)
        cp_ref[...] = jnp.zeros_like(cp_ref)

    x = x_ref[...]
    psi = expand_rows(ls_ref[...], lf_ref[...], rows, step * rows)
    acc[0:rank_l, :] += dot(psi, x, ((1,), (0,)))
    rt_ref[0] = dot(omega[...], x, ((1,), (1,)))

    @pl.when(step == pl.num_programs(0) - 1)
    def _():
        left = acc[...]
        hi = left.astype(BF16)
        rest = left - hi.astype(F32)
        mid = rest.astype(BF16)
        low = (rest - mid.astype(F32)).astype(BF16)
        dims = ((1,), (1,))
        om = omega[...]
        cp_ref[:, 0:rank_r] = dot(hi, om, dims) + (dot(mid, om, dims) + dot(low, om, dims))
        left_t = left.T
        for j in range(samples // 8):
            lt_ref[j % 2, j // (2 * NZ), (j // 2) % NZ] = left_t[8 * j : 8 * j + 8, :]


def exchange_kernel(
    nx,
    rt, lt, cp,
    c_out, l_out, r_out,
    cc, lc, cs, ls, cy, ly, cq, cz, cr, cx, cf, lz, lq, ra, rb, rl, rr,
    ssem, rsem,
):
    cell = lax.axis_index("cells")
    x = lax.axis_index("samp")
    c = lax.rem(cell, 2)
    z = lax.rem(cell // 2, NZ)
    y = cell // (2 * NZ)

    def at(y_, z_, c_, x_):
        return ((y_ * NZ + z_) * 2 + c_, x_)

    other = at(y, z, 1 - c, x)
    ys = [lax.rem(y + d, NY) for d in range(1, NY)]
    zs = [lax.rem(z + d, NZ) for d in range(1, NZ)]
    xs = [lax.rem(x + d, nx) for d in range(1, nx)]
    to_y = [at(p, z, c, x) for p in ys]
    to_z = [at(y, p, c, x) for p in zs]
    to_x = [at(y, z, c, p) for p in xs]

    barrier = pltpu.get_barrier_semaphore()
    peers = [other] + to_y + to_z + to_x
    for peer in peers:
        pl.semaphore_signal(barrier, inc=1, device_id=peer, device_id_type=MESH)
    pl.semaphore_wait(barrier, len(peers))

    used = [0]
    sent = []

    def send(src, dst, peer):
        k = used[0]
        used[0] += 1
        copy = pltpu.make_async_remote_copy(
            src_ref=src, dst_ref=dst, send_sem=ssem.at[k], recv_sem=rsem.at[k],
            device_id=peer, device_id_type=MESH,
        )
        copy.start()
        sent.append(copy)
        return copy

    def arrived(copies):
        for copy in copies:
            copy.wait_recv()

    half = rt.shape[2] // 2
    lo, hi = pl.ds(0, half), pl.ds(half, half)
    right, left = to_x[0], to_x[-1]

    g_cc = [send(cp.at[1 - c], cc, other)]
    g_lc = [send(lt.at[1 - c], lc, other)]
    far = lax.rem(x + 2, nx)
    g_ra = [send(rt.at[far, :, lo], ra, right)]
    g_rb = [send(rt.at[far, :, hi], rb, left)]

    arrived(g_cc)
    cs[...] = cp[c] + cc[...]
    g_cy = [send(cs.at[ys[i]], cy.at[i], to_y[i]) for i in range(NY - 1)]

    arrived(g_lc)
    ls[...] = lt[c] + lc[...]
    g_ly = [send(ls.at[ys[i]], ly.at[i], to_y[i]) for i in range(NY - 1)]

    arrived(g_ra)
    xr, xl = xs[0], xs[-1]
    rl[:, lo] = rt[xr, :, lo] + ra[...]
    rl[:, hi] = rt[xr, :, hi]
    arrived(g_rb)
    rr[:, lo] = rt[xl, :, lo]
    rr[:, hi] = rt[xl, :, hi] + rb[...]
    from_left, from_right = cx_refs = (r_out.at[0], r_out.at[1])
    g_r = [send(rl, from_left, right), send(rr, from_right, left)]

    arrived(g_cy)
    cq[...] = cs[y] + functools.reduce(lambda a, b: a + b, [cy[i] for i in range(NY - 1)])
    g_cz = [send(cq, cz.at[i], to_z[i]) for i in range(NZ - 1)]
    arrived(g_cz)
    cr[...] = cq[...] + functools.reduce(lambda a, b: a + b, [cz[i] for i in range(NZ - 1)])
    g_cx = [send(cr, cx.at[i], to_x[i]) for i in range(nx - 1)]
    arrived(g_cx)
    cf[c, y] = cr[...] + functools.reduce(lambda a, b: a + b, [cx[i] for i in range(nx - 1)])
    g_ag = [send(cf.at[c, y], cf.at[c, y], to_y[i]) for i in range(NY - 1)]

    arrived(g_ly)
    lq[...] = ls[y] + functools.reduce(lambda a, b: a + b, [ly[i] for i in range(NY - 1)])
    g_lz = [send(lq.at[zs[i]], lz.at[i], to_z[i]) for i in range(NZ - 1)]

    arrived(g_ag)
    g_ac = [send(cf.at[c], cf.at[c], other)]

    arrived(g_lz)
    l_out[...] = lq[z] + functools.reduce(lambda a, b: a + b, [lz[i] for i in range(NZ - 1)])
    arrived(g_r)
    r_out[2] = rt[x]
    arrived(g_ac)
    c_out[...] = cf[...]
    for copy in sent:
        copy.wait_send()


def rows_of(a, t):
    return jnp.broadcast_to(a[t : t + 1, :], (8, LP))


def lanes_of(a, t):
    return jnp.broadcast_to(a[:, t : t + 1], (8, LP))


def solve_kernel(rank_l, c_ref, l_ref, r_ref, core_ref, range_ref):
    cm = c_ref[...]
    gram = dot(cm, cm, ((1,), (1,)), HIGHEST)
    row = lax.broadcasted_iota(jnp.int32, (LP, LP), 0)
    col = lax.broadcasted_iota(jnp.int32, (LP, LP), 1)
    gram = gram + jnp.where(row == col, 0.5, 0.0)
    sub = lax.broadcasted_iota(jnp.int32, (8, LP), 0)
    lane = lax.broadcasted_iota(jnp.int32, (8, LP), 1)

    tiles = [gram[8 * i : 8 * i + 8, :] for i in range(LP // 8)]
    rhs = l_ref[...]
    panels = rank_l // 8
    for kb in range(panels):
        base = 8 * kb
        p = tiles[kb]
        cols = [lanes_of(p, base + t) for t in range(8)]
        for t in range(8):
            ct = cols[t]
            inv = 1.0 / rows_of(ct, t)
            here = lane == base + t
            prow = jnp.where(here, inv, rows_of(p, t) * inv)
            p = jnp.where(sub == t, prow, jnp.where(here, 0.0, p) - ct * prow)
            for j in range(t + 1, 8):
                crow = rows_of(cols[j], t) * inv
                cols[j] = jnp.where(sub == t, crow, cols[j] - ct * crow)
        inside = (lane >= base) & (lane < base + 8)
        w = jnp.where(inside, -p, p)
        ws = [rows_of(w, t) for t in range(8)]

        def update(a):
            terms = [lanes_of(a, base + t) * ws[t] for t in range(8)]
            while len(terms) > 1:
                terms = [terms[i] + terms[i + 1] for i in range(0, len(terms), 2)]
            return jnp.where(inside, 0.0, a) - terms[0]

        for i in range(kb + 1, panels):
            tiles[i] = update(tiles[i])
        rhs = update(rhs)
    core = dot(rhs, cm, ((1,), (0,)), HIGHEST)
    core_ref[...] = core[:, 0 : core_ref.shape[1]]
    range_ref[...] = r_ref[2] + (r_ref[0] + r_ref[1])


VMEM = pl.BlockSpec(memory_space=pltpu.VMEM)


def on_device(snapshots, left_slow, left_fast, right_slow, right_fast):
    nx = lax.axis_size("samp")
    rows, samples = snapshots.shape
    rank_l, rank_r = left_slow.shape[0], right_slow.shape[0]
    part = rows // nx
    pr = LP // (2 * NY)
    whole = lambda a: pl.BlockSpec(a.shape, lambda i: (0,) * len(a.shape))
    f32 = lambda *shape: jax.ShapeDtypeStruct(shape, F32)
    small = [left_slow.T, left_fast.T, right_slow.T, right_fast.T]
    lt_shape, cp_shape = f32(2, NY, NZ, 8, LP), f32(LP, RP)
    rt, lt, cp = pl.pallas_call(
        compute_kernel,
        grid=(nx,),
        in_specs=[pl.BlockSpec((part, samples), lambda i: (i, 0))] + [whole(a) for a in small],
        out_specs=(
            pl.BlockSpec((1, rank_r, part), lambda i: (i, 0, 0)),
            whole(lt_shape),
            whole(cp_shape),
        ),
        out_shape=(f32(nx, rank_r, part), lt_shape, cp_shape),
        scratch_shapes=[pltpu.VMEM((rank_r, samples), BF16), pltpu.VMEM((LP, samples), F32)],
        name="sketch",
    )(snapshots, *small)

    copies = 2 + 4 + 3 * (NY - 1) + 2 * (NZ - 1) + (nx - 1) + 1
    vm = lambda *shape: pltpu.VMEM(shape, F32)
    cf, lf, rf = pl.pallas_call(
        functools.partial(exchange_kernel, nx),
        in_specs=[VMEM] * 3,
        out_specs=(VMEM,) * 3,
        out_shape=(f32(2, NY, pr, RP), f32(8, LP), f32(3, rank_r, part)),
        scratch_shapes=[
            vm(NY, pr, RP), vm(NY, NZ, 8, LP), vm(NY, pr, RP), vm(NY, NZ, 8, LP),
            vm(NY - 1, pr, RP), vm(NY - 1, NZ, 8, LP),
            vm(pr, RP), vm(NZ - 1, pr, RP), vm(pr, RP), vm(nx - 1, pr, RP), vm(2, NY, pr, RP),
            vm(NZ - 1, 8, LP), vm(NZ, 8, LP),
            vm(rank_r, part // 2), vm(rank_r, part // 2), vm(rank_r, part), vm(rank_r, part),
            pltpu.SemaphoreType.DMA((copies,)), pltpu.SemaphoreType.DMA((copies,)),
        ],
        compiler_params=pltpu.CompilerParams(collective_id=0, has_side_effects=True),
        name="exchange",
    )(rt, lt, cp.reshape(2, NY, pr, RP))

    core_t, range_t = pl.pallas_call(
        functools.partial(solve_kernel, rank_l),
        in_specs=[VMEM] * 3,
        out_specs=(VMEM,) * 2,
        out_shape=(f32(8, rank_r), f32(rank_r, part)),
        name="solve",
    )(cf.reshape(LP, RP), lf, rf)
    return (range_t.T, core_t.T)


def solution(mesh):
    placed = (P("cells", "samp"), P(None, "cells"), P(), P(None, "samp"), P())
    return jax.shard_map(
        on_device,
        mesh=mesh,
        in_specs=placed,
        out_specs=(P(("cells", "samp"), None), P(None, ("samp", "cells"))),
        check_vma=False,
    )
```

```python
import functools

import jax
import jax.numpy as jnp
from jax import lax
from jax.experimental import pallas as pl
from jax.experimental.pallas import tpu as pltpu
from jax.sharding import PartitionSpec as P

F32 = jnp.float32
BF16 = jnp.bfloat16
MESH = pl.DeviceIdType.MESH
NY, NZ = 8, 8
LP = 128
HIGHEST = lax.Precision.HIGHEST


def dot(a, b, dims, precision=None):
    return lax.dot_general(a, b, (dims, ((), ())), precision=precision, preferred_element_type=F32)


def total(terms):
    return functools.reduce(lambda a, b: a + b, terms)


def expand_rows(slow_t, fast_t, width):
    ns, nf = slow_t.shape[0], fast_t.shape[0]
    n = lax.broadcasted_iota(jnp.int32, (ns, width), 1)
    a = lax.broadcasted_iota(jnp.int32, (ns, width), 0)
    pick_slow = jnp.where(n // nf == a, 1.0, 0.0).astype(BF16)
    n = lax.broadcasted_iota(jnp.int32, (nf, width), 1)
    b = lax.broadcasted_iota(jnp.int32, (nf, width), 0)
    pick_fast = jnp.where(n % nf == b, 1.0, 0.0).astype(BF16)
    dims = ((0,), (0,))
    return (dot(slow_t, pick_slow, dims) * dot(fast_t, pick_fast, dims)).astype(BF16)


def sketch_kernel(
    nx, part,
    x_hbm, ls_ref, lf_ref, rs_ref, rf_ref,
    c_out, l_out, r_out,
    xb, psi, omega, acc, ct, rt, lt, cp,
    cc, cs, cy, cq, cz, cr, cx, cf,
    lc, ls, ly, lq, lz,
    ra, rb, rl, rr,
    xsem, ssem, rsem, osem,
):
    cell = lax.axis_index("cells")
    x = lax.axis_index("samp")
    c = lax.rem(cell, 2)
    z = lax.rem(cell // 2, NZ)
    y = cell // (2 * NZ)
    rank_l, rank_r = ls_ref.shape[1], rs_ref.shape[1]
    rows, samples = xb.shape
    pr = cp.shape[2]

    def at(y_, z_, c_, x_):
        return ((y_ * NZ + z_) * 2 + c_, x_)

    other = at(y, z, 1 - c, x)
    ys = [lax.rem(y + d, NY) for d in range(1, NY)]
    zs = [lax.rem(z + d, NZ) for d in range(1, NZ)]
    xs = [lax.rem(x + d, nx) for d in range(1, nx)]
    to_y = [at(p, z, c, x) for p in ys]
    to_z = [at(y, p, c, x) for p in zs]
    to_x = [at(y, z, c, p) for p in xs]
    right, left = to_x[0], to_x[-1]

    loads = []
    for i in range(nx):
        span = pl.ds(i * part, part)
        loads.append(pltpu.make_async_copy(x_hbm.at[span], xb.at[span], xsem.at[i]))
        loads[-1].start()

    barrier = pltpu.get_barrier_semaphore()
    peers = [other] + to_y + to_z + to_x
    for peer in peers:
        pl.semaphore_signal(barrier, inc=1, device_id=peer, device_id_type=MESH)

    used = [0]
    sent = []

    def remote(src, dst, peer):
        k = used[0]
        used[0] += 1
        copy = pltpu.make_async_remote_copy(
            src_ref=src, dst_ref=dst, send_sem=ssem.at[k], recv_sem=rsem.at[k],
            device_id=peer, device_id_type=MESH,
        )
        sent.append(copy)
        return copy

    def send(src, dst, peer):
        copy = remote(src, dst, peer)
        copy.start()
        return copy

    def arrived(copies):
        for copy in copies:
            copy.wait_recv()

    early = z < NZ // 2
    half = part // 2
    lo, hi = pl.ds(0, half), pl.ds(half, half)
    far = lax.rem(x + 2, nx)
    g_ra = remote(rt.at[far, :, lo], ra, right)
    g_rb = remote(rt.at[far, :, hi], rb, left)

    def range_product():
        for i in range(nx):
            rt[i] = dot(omega[...], xb[i * part : (i + 1) * part, :], ((1,), (1,)))

    def range_start():
        g_ra.start()
        g_rb.start()

    psi[...] = expand_rows(ls_ref[...], lf_ref[...], rows)
    omega[...] = expand_rows(rs_ref[...], rf_ref[...], samples)
    for copy in loads:
        copy.wait()

    @pl.when(early)
    def _():
        range_product()

    left_part = dot(psi[...], xb[...], ((1,), (0,)))
    acc[rank_l:, :] = jnp.zeros((LP - rank_l, samples), F32)
    acc[0:rank_l, :] = left_part
    top = left_part.astype(BF16)
    rest = left_part - top.astype(F32)
    mid = rest.astype(BF16)
    low = (rest - mid.astype(F32)).astype(BF16)
    om = omega[...]
    dims = ((1,), (1,))
    ct[...] = jnp.zeros_like(ct)
    ct[0:rank_r, 0:rank_l] = dot(om, top, dims) + (dot(om, mid, dims) + dot(om, low, dims))
    for k in range(2 * NY):
        cp[k // NY, k % NY] = ct[k * pr : (k + 1) * pr, :]

    pl.semaphore_wait(barrier, len(peers))
    g_cc = [send(cp.at[1 - c], cc, other)]

    @pl.when(early)
    def _():
        range_start()

    left_t = acc[...].T
    for j in range(samples // 8):
        lt[j % 2, j // (2 * NZ), (j // 2) % NZ] = left_t[8 * j : 8 * j + 8, :]
    g_lc = [send(lt.at[1 - c], lc, other)]

    arrived(g_cc)
    cs[...] = cp[c] + cc[...]
    g_cy = [send(cs.at[ys[i]], cy.at[i], to_y[i]) for i in range(NY - 1)]

    @pl.when(jnp.logical_not(early))
    def _():
        range_product()
        range_start()

    arrived(g_lc)
    ls[...] = lt[c] + lc[...]
    g_ly = [send(ls.at[ys[i]], ly.at[i], to_y[i]) for i in range(NY - 1)]

    arrived(g_cy)
    cq[...] = cs[y] + total([cy[i] for i in range(NY - 1)])
    g_cz = [send(cq, cz.at[i], to_z[i]) for i in range(NZ - 1)]

    arrived([g_ra, g_rb])
    xr, xl = xs[0], xs[-1]
    rl[:, lo] = rt[xr, :, lo] + ra[...]
    rl[:, hi] = rt[xr, :, hi]
    rr[:, lo] = rt[xl, :, lo]
    rr[:, hi] = rt[xl, :, hi] + rb[...]
    g_r = [send(rl, r_out.at[0], right), send(rr, r_out.at[1], left)]
    own = pltpu.make_async_copy(rt.at[x], r_out.at[2], osem)
    own.start()

    arrived(g_cz)
    cr[...] = cq[...] + total([cz[i] for i in range(NZ - 1)])
    g_cx = [send(cr, cx.at[i], to_x[i]) for i in range(nx - 1)]
    arrived(g_cx)
    cf[c, y] = cr[...] + total([cx[i] for i in range(nx - 1)])
    g_ag = [send(cf.at[c, y], cf.at[c, y], to_y[i]) for i in range(NY - 1)]

    arrived(g_ly)
    lq[...] = ls[y] + total([ly[i] for i in range(NY - 1)])
    g_lz = [send(lq.at[zs[i]], lz.at[i], to_z[i]) for i in range(NZ - 1)]

    arrived(g_ag)
    g_ac = [send(cf.at[c], cf.at[c], other)]

    arrived(g_lz)
    l_out[...] = lq[z] + total([lz[i] for i in range(NZ - 1)])
    arrived(g_ac)
    c_out[...] = cf[...]
    own.wait()
    arrived(g_r)
    for copy in sent:
        copy.wait_send()


def rows_of(a, t):
    return jnp.broadcast_to(a[t : t + 1, :], (8, LP))


def lanes_of(a, t):
    return jnp.broadcast_to(a[:, t : t + 1], (8, LP))


def solve_kernel(rank_l, c_ref, l_ref, r_hbm, core_ref, range_hbm, ct, rbuf, rsum, rsem, wsem):
    fetch = pltpu.make_async_copy(r_hbm, rbuf, rsem)
    fetch.start()
    pr = c_ref.shape[2]
    for k in range(2 * NY):
        ct[k * pr : (k + 1) * pr, :] = c_ref[k // NY, k % NY]
    cm = ct[...]
    gram = dot(cm, cm, ((0,), (0,)), HIGHEST)
    row = lax.broadcasted_iota(jnp.int32, (LP, LP), 0)
    col = lax.broadcasted_iota(jnp.int32, (LP, LP), 1)
    gram = gram + jnp.where(row == col, 0.5, 0.0)
    sub = lax.broadcasted_iota(jnp.int32, (8, LP), 0)
    lane = lax.broadcasted_iota(jnp.int32, (8, LP), 1)

    fetch.wait()
    rsum[...] = rbuf[2] + (rbuf[0] + rbuf[1])
    write = pltpu.make_async_copy(rsum, range_hbm, wsem)
    write.start()

    tiles = [gram[8 * i : 8 * i + 8, :] for i in range(LP // 8)]
    rhs = l_ref[...]
    panels = rank_l // 8
    for kb in range(panels):
        base = 8 * kb
        p = tiles[kb]
        cols = [lanes_of(p, base + t) for t in range(8)]
        for t in range(8):
            ct_ = cols[t]
            inv = 1.0 / rows_of(ct_, t)
            here = lane == base + t
            prow = jnp.where(here, inv, rows_of(p, t) * inv)
            p = jnp.where(sub == t, prow, jnp.where(here, 0.0, p) - ct_ * prow)
            for j in range(t + 1, 8):
                crow = rows_of(cols[j], t) * inv
                cols[j] = jnp.where(sub == t, crow, cols[j] - ct_ * crow)
        inside = (lane >= base) & (lane < base + 8)
        w = jnp.where(inside, -p, p)
        ws = [rows_of(w, t) for t in range(8)]

        def update(a):
            terms = [lanes_of(a, base + t) * ws[t] for t in range(8)]
            while len(terms) > 1:
                terms = [terms[i] + terms[i + 1] for i in range(0, len(terms), 2)]
            return jnp.where(inside, 0.0, a) - terms[0]

        for i in range(kb + 1, panels):
            tiles[i] = update(tiles[i])
        rhs = update(rhs)
    core = dot(rhs, cm, ((1,), (1,)), HIGHEST)
    core_ref[...] = core[:, 0 : core_ref.shape[1]]
    write.wait()


VMEM = pl.BlockSpec(memory_space=pltpu.VMEM)
ANY = pl.BlockSpec(memory_space=pl.ANY)


def on_device(snapshots, left_slow, left_fast, right_slow, right_fast):
    nx = lax.axis_size("samp")
    rows, samples = snapshots.shape
    rank_l, rank_r = left_slow.shape[0], right_slow.shape[0]
    part = rows // nx
    pr = -(-rank_r // (2 * NY))
    f32 = lambda *shape: jax.ShapeDtypeStruct(shape, F32)
    vm = lambda *shape: pltpu.VMEM(shape, F32)
    dma = lambda *shape: pltpu.SemaphoreType.DMA(shape)
    copies = 2 + 4 + 3 * (NY - 1) + 2 * (NZ - 1) + (nx - 1) + 1
    cf, lf, rf = pl.pallas_call(
        functools.partial(sketch_kernel, nx, part),
        in_specs=[ANY] + [VMEM] * 4,
        out_specs=(VMEM, VMEM, ANY),
        out_shape=(f32(2, NY, pr, LP), f32(8, LP), f32(3, rank_r, part)),
        scratch_shapes=[
            pltpu.VMEM((rows, samples), BF16),
            pltpu.VMEM((rank_l, rows), BF16),
            pltpu.VMEM((rank_r, samples), BF16),
            vm(LP, samples), vm(2 * NY * pr, LP), vm(nx, rank_r, part),
            vm(2, NY, NZ, 8, LP), vm(2, NY, pr, LP),
            vm(NY, pr, LP), vm(NY, pr, LP), vm(NY - 1, pr, LP), vm(pr, LP),
            vm(NZ - 1, pr, LP), vm(pr, LP), vm(nx - 1, pr, LP), vm(2, NY, pr, LP),
            vm(NY, NZ, 8, LP), vm(NY, NZ, 8, LP), vm(NY - 1, NZ, 8, LP), vm(NZ, 8, LP),
            vm(NZ - 1, 8, LP),
            vm(rank_r, part // 2), vm(rank_r, part // 2), vm(rank_r, part), vm(rank_r, part),
            dma(nx), dma(copies), dma(copies), pltpu.SemaphoreType.DMA,
        ],
        compiler_params=pltpu.CompilerParams(collective_id=0, has_side_effects=True),
        name="sketch",
    )(snapshots, left_slow.T, left_fast.T, right_slow.T, right_fast.T)

    core_t, range_t = pl.pallas_call(
        functools.partial(solve_kernel, rank_l),
        in_specs=[VMEM, VMEM, ANY],
        out_specs=(VMEM, ANY),
        out_shape=(f32(8, rank_r), f32(rank_r, part)),
        scratch_shapes=[
            vm(2 * NY * pr, LP), vm(3, rank_r, part), vm(rank_r, part),
            pltpu.SemaphoreType.DMA, pltpu.SemaphoreType.DMA,
        ],
        name="solve",
    )(cf, lf, rf)
    return (range_t.T, core_t.T)


def solution(mesh):
    placed = (P("cells", "samp"), P(None, "cells"), P(), P(None, "samp"), P())
    return jax.shard_map(
        on_device,
        mesh=mesh,
        in_specs=placed,
        out_specs=(P(("cells", "samp"), None), P(None, ("samp", "cells"))),
        check_vma=False,
    )
```

```python
import functools

import jax
import jax.numpy as jnp
from jax import lax
from jax.experimental import pallas as pl
from jax.experimental.pallas import tpu as pltpu
from jax.sharding import PartitionSpec as P

F32 = jnp.float32
BF16 = jnp.bfloat16
MESH = pl.DeviceIdType.MESH
NY, NZ = 8, 8
LP = 128
HIGHEST = lax.Precision.HIGHEST


def dot(a, b, dims, precision=None):
    return lax.dot_general(a, b, (dims, ((), ())), precision=precision, preferred_element_type=F32)


def total(terms):
    return functools.reduce(lambda a, b: a + b, terms)


def expand_rows(slow_t, fast_t, width):
    ns, nf = slow_t.shape[0], fast_t.shape[0]
    n = lax.broadcasted_iota(jnp.int32, (ns, width), 1)
    a = lax.broadcasted_iota(jnp.int32, (ns, width), 0)
    pick_slow = jnp.where(n // nf == a, 1.0, 0.0).astype(BF16)
    n = lax.broadcasted_iota(jnp.int32, (nf, width), 1)
    b = lax.broadcasted_iota(jnp.int32, (nf, width), 0)
    pick_fast = jnp.where(n % nf == b, 1.0, 0.0).astype(BF16)
    dims = ((0,), (0,))
    return (dot(slow_t, pick_slow, dims) * dot(fast_t, pick_fast, dims)).astype(BF16)


def sketch_kernel(
    nx, part,
    x_hbm, ls_hbm, lf_hbm, rs_hbm, rf_hbm,
    c_out, l_out, r_out,
    ls_ref, lf_ref, rs_ref, rf_ref, xb, psi, omega, acc, ct, rt, lt, cp,
    cy, cq, cx, cr, cz, cw,
    lc, ls, ly, lq, lz, lw,
    ra, rb, rl, rr,
    xsem, wsem, ssem, rsem, osem,
):
    cell = lax.axis_index("cells")
    x = lax.axis_index("samp")
    c = lax.rem(cell, 2)
    z = lax.rem(cell // 2, NZ)
    y = cell // (2 * NZ)
    rank_l, rank_r = ls_ref.shape[1], rs_ref.shape[1]
    samples = xb.shape[1]
    pr = cp.shape[2]

    def at(y_, z_, c_, x_):
        return ((y_ * NZ + z_) * 2 + c_, x_)

    ys = [lax.rem(y + d, NY) for d in range(1, NY)]
    zs = [lax.rem(z + d, NZ) for d in range(1, NZ)]
    xs = [lax.rem(x + d, nx) for d in range(1, nx)]
    other = at(y, z, 1 - c, x)
    to_y = [at(p, z, c, x) for p in ys]
    to_yc = [at(p, z, 1 - c, x) for p in ys]
    to_z = [at(y, p, c, x) for p in zs]
    to_x = [at(y, z, c, p) for p in xs]
    right, left = to_x[0], to_x[-1]

    barrier = pltpu.get_barrier_semaphore()
    peers = [other] + to_y + to_yc + to_z + to_x
    for peer in peers:
        pl.semaphore_signal(barrier, inc=1, device_id=peer, device_id_type=MESH)

    small = [
        pltpu.make_async_copy(src, dst, wsem.at[i])
        for i, (src, dst) in enumerate(
            [(ls_hbm, ls_ref), (lf_hbm, lf_ref), (rs_hbm, rs_ref), (rf_hbm, rf_ref)]
        )
    ]
    loads = []
    for i in range(nx):
        span = pl.ds(i * part, part)
        loads.append(pltpu.make_async_copy(x_hbm.at[span], xb.at[span], xsem.at[i]))
    for copy in small + loads:
        copy.start()

    used = [0]
    sent = []

    def remote(src, dst, peer):
        k = used[0]
        used[0] += 1
        copy = pltpu.make_async_remote_copy(
            src_ref=src, dst_ref=dst, send_sem=ssem.at[k], recv_sem=rsem.at[k],
            device_id=peer, device_id_type=MESH,
        )
        sent.append(copy)
        return copy

    def send(src, dst, peer):
        copy = remote(src, dst, peer)
        copy.start()
        return copy

    def arrived(copies):
        for copy in copies:
            copy.wait_recv()

    early = z < NZ // 2
    late = jnp.logical_not(early)
    half = part // 2
    lo, hi = pl.ds(0, half), pl.ds(half, half)
    far = lax.rem(x + 2, nx)
    xr, xl = xs[0], xs[-1]
    g_ra = [remote(rt.at[far, :, lo], ra, right), remote(rt.at[far, :, hi], rb, left)]
    g_r = [remote(rl, r_out.at[0], right), remote(rr, r_out.at[1], left)]
    own_r = pltpu.make_async_copy(rt.at[x], r_out.at[2], osem.at[0])

    def range_product():
        for i in range(nx):
            rt[i] = dot(omega[...], xb[i * part : (i + 1) * part, :], ((1,), (1,)))

    def range_first():
        for copy in g_ra:
            copy.start()
        own_r.start()

    def range_second():
        arrived(g_ra)
        rl[:, lo] = rt[xr, :, lo] + ra[...]
        rl[:, hi] = rt[xr, :, hi]
        rr[:, lo] = rt[xl, :, lo]
        rr[:, hi] = rt[xl, :, hi] + rb[...]
        for copy in g_r:
            copy.start()

    for copy in small:
        copy.wait()
    omega[...] = expand_rows(rs_ref[...], rf_ref[...], samples)
    psi[...] = expand_rows(ls_ref[...], lf_ref[...], nx * part)
    acc[rank_l:, :] = jnp.zeros((LP - rank_l, samples), F32)
    for i in range(nx):
        loads[i].wait()
        rows = slice(i * part, (i + 1) * part)
        term = dot(psi[:, rows], xb[rows, :], ((1,), (0,)))
        acc[0:rank_l, :] = term if i == 0 else acc[0:rank_l, :] + term

    left_part = acc[0:rank_l, :]
    top = left_part.astype(BF16)
    rest = left_part - top.astype(F32)
    mid = rest.astype(BF16)
    low = (rest - mid.astype(F32)).astype(BF16)
    om = omega[...]
    dims = ((1,), (1,))
    ct[...] = jnp.zeros_like(ct)
    ct[0:rank_r, 0:rank_l] = dot(om, top, dims) + (dot(om, mid, dims) + dot(om, low, dims))
    for k in range(2 * NY):
        cp[k // NY, k % NY] = ct[k * pr : (k + 1) * pr, :]

    @pl.when(early)
    def _():
        range_product()

    pl.semaphore_wait(barrier, len(peers))

    g_cy = [send(cp.at[c, ys[i]], cy.at[i], to_y[i]) for i in range(NY - 1)]
    g_cy += [send(cp.at[1 - c, ys[i]], cy.at[NY - 1 + i], to_yc[i]) for i in range(NY - 1)]
    g_cy += [send(cp.at[1 - c, y], cy.at[2 * NY - 2], other)]

    @pl.when(early)
    def _():
        range_first()

    left_t = acc[...].T
    for j in range(samples // 8):
        lt[j % 2, j // (2 * NZ), (j // 2) % NZ] = left_t[8 * j : 8 * j + 8, :]
    g_lc = [send(lt.at[1 - c], lc, other)]

    @pl.when(late)
    def _():
        range_product()

    arrived(g_lc)
    ls[...] = lt[c] + lc[...]

    @pl.when(early)
    def _():
        range_second()

    arrived(g_cy)
    cq[...] = cp[c, y] + total([cy[i] for i in range(2 * NY - 1)])
    g_cx = [send(cq, cx.at[i], to_x[i]) for i in range(nx - 1)]

    @pl.when(late)
    def _():
        range_first()

    g_ly = [send(ls.at[ys[i]], ly.at[i], to_y[i]) for i in range(NY - 1)]

    arrived(g_cx)
    cr[...] = cq[...] + total([cx[i] for i in range(nx - 1)])
    g_cz = [send(cr, cz.at[i], to_z[i]) for i in range(NZ - 1)]

    @pl.when(late)
    def _():
        range_second()

    arrived(g_cz)
    cw[...] = cr[...] + total([cz[i] for i in range(NZ - 1)])
    g_ag = [send(cw, c_out.at[c, y], to_y[i]) for i in range(NY - 1)]
    g_ag += [send(cw, c_out.at[c, y], to_yc[i]) for i in range(NY - 1)]
    g_ag += [send(cw, c_out.at[c, y], other)]
    own_c = pltpu.make_async_copy(cw, c_out.at[c, y], osem.at[1])
    own_c.start()

    arrived(g_ly)
    lq[...] = ls[y] + total([ly[i] for i in range(NY - 1)])
    g_lz = [send(lq.at[zs[i]], lz.at[i], to_z[i]) for i in range(NZ - 1)]
    arrived(g_lz)
    lw[...] = lq[z] + total([lz[i] for i in range(NZ - 1)])
    own_l = pltpu.make_async_copy(lw, l_out, osem.at[2])
    own_l.start()

    own_r.wait()
    own_c.wait()
    arrived(g_r)
    arrived(g_ag)
    own_l.wait()
    for copy in sent:
        copy.wait_send()


def rows_of(a, t):
    return jnp.broadcast_to(a[t : t + 1, :], (8, LP))


def lanes_of(a, t):
    return jnp.broadcast_to(a[:, t : t + 1], (8, LP))


def solve_kernel(rank_l, c_ref, l_ref, r_hbm, core_ref, range_hbm, ct, rbuf, rsum, rsem, wsem):
    fetch = pltpu.make_async_copy(r_hbm, rbuf, rsem)
    fetch.start()
    pr = c_ref.shape[2]
    for k in range(2 * NY):
        ct[k * pr : (k + 1) * pr, :] = c_ref[k // NY, k % NY]
    cm = ct[...]
    gram = dot(cm, cm, ((0,), (0,)), HIGHEST)
    row = lax.broadcasted_iota(jnp.int32, (LP, LP), 0)
    col = lax.broadcasted_iota(jnp.int32, (LP, LP), 1)
    gram = gram + jnp.where(row == col, 0.5, 0.0)
    sub = lax.broadcasted_iota(jnp.int32, (8, LP), 0)
    lane = lax.broadcasted_iota(jnp.int32, (8, LP), 1)

    fetch.wait()
    rsum[...] = rbuf[2] + (rbuf[0] + rbuf[1])
    write = pltpu.make_async_copy(rsum, range_hbm, wsem)
    write.start()

    tiles = [gram[8 * i : 8 * i + 8, :] for i in range(LP // 8)]
    rhs = l_ref[...]
    panels = rank_l // 8
    for kb in range(panels):
        base = 8 * kb
        p = tiles[kb]
        cols = [lanes_of(p, base + t) for t in range(8)]
        for t in range(8):
            ct_ = cols[t]
            inv = 1.0 / rows_of(ct_, t)
            here = lane == base + t
            prow = jnp.where(here, inv, rows_of(p, t) * inv)
            p = jnp.where(sub == t, prow, jnp.where(here, 0.0, p) - ct_ * prow)
            for j in range(t + 1, 8):
                crow = rows_of(cols[j], t) * inv
                cols[j] = jnp.where(sub == t, crow, cols[j] - ct_ * crow)
        inside = (lane >= base) & (lane < base + 8)
        w = jnp.where(inside, -p, p)
        ws = [rows_of(w, t) for t in range(8)]

        def update(a):
            terms = [lanes_of(a, base + t) * ws[t] for t in range(8)]
            while len(terms) > 1:
                terms = [terms[i] + terms[i + 1] for i in range(0, len(terms), 2)]
            return jnp.where(inside, 0.0, a) - terms[0]

        for i in range(kb + 1, panels):
            tiles[i] = update(tiles[i])
        rhs = update(rhs)
    core = dot(rhs, cm, ((1,), (1,)), HIGHEST)
    core_ref[...] = core[:, 0 : core_ref.shape[1]]
    write.wait()


VMEM = pl.BlockSpec(memory_space=pltpu.VMEM)
ANY = pl.BlockSpec(memory_space=pl.ANY)


def on_device(snapshots, left_slow, left_fast, right_slow, right_fast):
    nx = lax.axis_size("samp")
    rows, samples = snapshots.shape
    rank_l, rank_r = left_slow.shape[0], right_slow.shape[0]
    part = rows // nx
    pr = -(-rank_r // (2 * NY))
    f32 = lambda *shape: jax.ShapeDtypeStruct(shape, F32)
    vm = lambda *shape: pltpu.VMEM(shape, F32)
    dma = lambda *shape: pltpu.SemaphoreType.DMA(shape)
    copies = 4 + 2 * (2 * NY - 1) + (nx - 1) + (NZ - 1) + 1 + (NY - 1) + (NZ - 1)
    small = [left_slow.T, left_fast.T, right_slow.T, right_fast.T]
    cf, lf, rf = pl.pallas_call(
        functools.partial(sketch_kernel, nx, part),
        in_specs=[ANY] * 5,
        out_specs=(ANY,) * 3,
        out_shape=(f32(2, NY, pr, LP), f32(8, LP), f32(3, rank_r, part)),
        scratch_shapes=[pltpu.VMEM(a.shape, BF16) for a in small] + [
            pltpu.VMEM((rows, samples), BF16),
            pltpu.VMEM((rank_l, rows), BF16),
            pltpu.VMEM((rank_r, samples), BF16),
            vm(LP, samples), vm(2 * NY * pr, LP), vm(nx, rank_r, part),
            vm(2, NY, NZ, 8, LP), vm(2, NY, pr, LP),
            vm(2 * NY - 1, pr, LP), vm(pr, LP), vm(nx - 1, pr, LP), vm(pr, LP),
            vm(NZ - 1, pr, LP), vm(pr, LP),
            vm(NY, NZ, 8, LP), vm(NY, NZ, 8, LP), vm(NY - 1, NZ, 8, LP), vm(NZ, 8, LP),
            vm(NZ - 1, 8, LP), vm(8, LP),
            vm(rank_r, part // 2), vm(rank_r, part // 2), vm(rank_r, part), vm(rank_r, part),
            dma(nx), dma(4), dma(copies), dma(copies), dma(3),
        ],
        compiler_params=pltpu.CompilerParams(collective_id=0, has_side_effects=True),
        name="sketch",
    )(snapshots, *small)

    core_t, range_t = pl.pallas_call(
        functools.partial(solve_kernel, rank_l),
        in_specs=[VMEM, VMEM, ANY],
        out_specs=(VMEM, ANY),
        out_shape=(f32(8, rank_r), f32(rank_r, part)),
        scratch_shapes=[
            vm(2 * NY * pr, LP), vm(3, rank_r, part), vm(rank_r, part),
            pltpu.SemaphoreType.DMA, pltpu.SemaphoreType.DMA,
        ],
        name="solve",
    )(cf, lf, rf)
    return (range_t.T, core_t.T)


def solution(mesh):
    placed = (P("cells", "samp"), P(None, "cells"), P(), P(None, "samp"), P())
    return jax.shard_map(
        on_device,
        mesh=mesh,
        in_specs=placed,
        out_specs=(P(("cells", "samp"), None), P(None, ("samp", "cells"))),
        check_vma=False,
    )
```

```python
import functools

import jax
import jax.numpy as jnp
from jax import lax
from jax.experimental import pallas as pl
from jax.experimental.pallas import tpu as pltpu
from jax.sharding import PartitionSpec as P

F32 = jnp.float32
BF16 = jnp.bfloat16
MESH = pl.DeviceIdType.MESH
NY, NZ = 8, 8
LP = 128
HIGHEST = lax.Precision.HIGHEST


def dot(a, b, dims, precision=None):
    return lax.dot_general(a, b, (dims, ((), ())), precision=precision, preferred_element_type=F32)


def total(terms):
    return functools.reduce(lambda a, b: a + b, terms)


def expand_rows(slow_t, fast_t, width):
    ns, nf = slow_t.shape[0], fast_t.shape[0]
    n = lax.broadcasted_iota(jnp.int32, (ns, width), 1)
    a = lax.broadcasted_iota(jnp.int32, (ns, width), 0)
    pick_slow = jnp.where(n // nf == a, 1.0, 0.0).astype(BF16)
    n = lax.broadcasted_iota(jnp.int32, (nf, width), 1)
    b = lax.broadcasted_iota(jnp.int32, (nf, width), 0)
    pick_fast = jnp.where(n % nf == b, 1.0, 0.0).astype(BF16)
    dims = ((0,), (0,))
    return (dot(slow_t, pick_slow, dims) * dot(fast_t, pick_fast, dims)).astype(BF16)


def sketch_kernel(
    nx, part,
    x_hbm, ls_hbm, lf_hbm, rs_hbm, rf_hbm,
    c_out, l_out, r_out,
    ls_ref, lf_ref, rs_ref, rf_ref, xb, psi, omega, acc, ct, rt, lt, cp,
    cy, cq, cx, cr, cz, cw,
    lc, ls, ly, lq, lz, lw,
    ra, rb, rl, rr, rf, rsum,
    xsem, wsem, ssem, rsem, osem,
):
    cell = lax.axis_index("cells")
    x = lax.axis_index("samp")
    c = lax.rem(cell, 2)
    z = lax.rem(cell // 2, NZ)
    y = cell // (2 * NZ)
    rank_l, rank_r = ls_ref.shape[1], rs_ref.shape[1]
    samples = xb.shape[1]
    pr = cp.shape[2]

    def at(y_, z_, c_, x_):
        return ((y_ * NZ + z_) * 2 + c_, x_)

    ys = [lax.rem(y + d, NY) for d in range(1, NY)]
    zs = [lax.rem(z + d, NZ) for d in range(1, NZ)]
    xs = [lax.rem(x + d, nx) for d in range(1, nx)]
    other = at(y, z, 1 - c, x)
    to_y = [at(p, z, c, x) for p in ys]
    to_yc = [at(p, z, 1 - c, x) for p in ys]
    to_z = [at(y, p, c, x) for p in zs]
    to_x = [at(y, z, c, p) for p in xs]
    right, left = to_x[0], to_x[-1]

    barrier = pltpu.get_barrier_semaphore()
    peers = [other] + to_y + to_yc + to_z + to_x
    for peer in peers:
        pl.semaphore_signal(barrier, inc=1, device_id=peer, device_id_type=MESH)

    small = [
        pltpu.make_async_copy(src, dst, wsem.at[i])
        for i, (src, dst) in enumerate(
            [(ls_hbm, ls_ref), (lf_hbm, lf_ref), (rs_hbm, rs_ref), (rf_hbm, rf_ref)]
        )
    ]
    loads = []
    for i in range(nx):
        span = pl.ds(i * part, part)
        loads.append(pltpu.make_async_copy(x_hbm.at[span], xb.at[span], xsem.at[i]))
    for copy in small + loads:
        copy.start()

    used = [0]
    sent = []

    def remote(src, dst, peer):
        k = used[0]
        used[0] += 1
        copy = pltpu.make_async_remote_copy(
            src_ref=src, dst_ref=dst, send_sem=ssem.at[k], recv_sem=rsem.at[k],
            device_id=peer, device_id_type=MESH,
        )
        sent.append(copy)
        return copy

    def send(src, dst, peer):
        copy = remote(src, dst, peer)
        copy.start()
        return copy

    def arrived(copies):
        for copy in copies:
            copy.wait_recv()

    early = z < NZ // 2
    late = jnp.logical_not(early)
    half = part // 2
    lo, hi = pl.ds(0, half), pl.ds(half, half)
    far = lax.rem(x + 2, nx)
    xr, xl = xs[0], xs[-1]
    g_ra = [remote(rt.at[far, :, lo], ra, right), remote(rt.at[far, :, hi], rb, left)]
    g_r = [remote(rl, rf.at[0], right), remote(rr, rf.at[1], left)]
    own_r = pltpu.make_async_copy(rsum, r_out, osem.at[0])

    def range_product():
        for i in range(nx):
            rt[i] = dot(omega[...], xb[i * part : (i + 1) * part, :], ((1,), (1,)))

    def range_first():
        for copy in g_ra:
            copy.start()

    def range_second():
        arrived(g_ra)
        rl[:, lo] = rt[xr, :, lo] + ra[...]
        rl[:, hi] = rt[xr, :, hi]
        rr[:, lo] = rt[xl, :, lo]
        rr[:, hi] = rt[xl, :, hi] + rb[...]
        for copy in g_r:
            copy.start()

    for copy in small:
        copy.wait()
    omega[...] = expand_rows(rs_ref[...], rf_ref[...], samples)
    psi[...] = expand_rows(ls_ref[...], lf_ref[...], nx * part)
    acc[rank_l:, :] = jnp.zeros((LP - rank_l, samples), F32)
    for i in range(nx):
        loads[i].wait()
        rows = slice(i * part, (i + 1) * part)
        term = dot(psi[:, rows], xb[rows, :], ((1,), (0,)))
        acc[0:rank_l, :] = term if i == 0 else acc[0:rank_l, :] + term

    left_part = acc[0:rank_l, :]
    top = left_part.astype(BF16)
    rest = left_part - top.astype(F32)
    mid = rest.astype(BF16)
    low = (rest - mid.astype(F32)).astype(BF16)
    om = omega[...]
    dims = ((1,), (1,))
    ct[...] = jnp.zeros_like(ct)
    ct[0:rank_r, 0:rank_l] = dot(om, top, dims) + (dot(om, mid, dims) + dot(om, low, dims))
    for k in range(2 * NY):
        cp[k // NY, k % NY] = ct[k * pr : (k + 1) * pr, :]

    @pl.when(early)
    def _():
        range_product()

    pl.semaphore_wait(barrier, len(peers))

    g_cy = [send(cp.at[c, ys[i]], cy.at[i], to_y[i]) for i in range(NY - 1)]
    g_cy += [send(cp.at[1 - c, ys[i]], cy.at[NY - 1 + i], to_yc[i]) for i in range(NY - 1)]
    g_cy += [send(cp.at[1 - c, y], cy.at[2 * NY - 2], other)]

    @pl.when(early)
    def _():
        range_first()

    left_t = acc[...].T
    for j in range(samples // 8):
        lt[j % 2, j // (2 * NZ), (j // 2) % NZ] = left_t[8 * j : 8 * j + 8, :]
    g_lc = [send(lt.at[1 - c], lc, other)]

    @pl.when(late)
    def _():
        range_product()

    arrived(g_lc)
    ls[...] = lt[c] + lc[...]

    arrived(g_cy)
    cq[...] = cp[c, y] + total([cy[i] for i in range(2 * NY - 1)])
    g_cx = [send(cq, cx.at[i], to_x[i]) for i in range(nx - 1)]

    @pl.when(early)
    def _():
        range_second()

    @pl.when(late)
    def _():
        range_first()

    g_ly = [send(ls.at[ys[i]], ly.at[i], to_y[i]) for i in range(NY - 1)]

    arrived(g_cx)
    cr[...] = cq[...] + total([cx[i] for i in range(nx - 1)])
    g_cz = [send(cr, cz.at[i], to_z[i]) for i in range(NZ - 1)]

    @pl.when(late)
    def _():
        range_second()

    arrived(g_cz)
    cw[...] = cr[...] + total([cz[i] for i in range(NZ - 1)])
    g_ag = [send(cw, c_out.at[c, y], to_y[i]) for i in range(NY - 1)]
    g_ag += [send(cw, c_out.at[c, y], to_yc[i]) for i in range(NY - 1)]
    g_ag += [send(cw, c_out.at[c, y], other)]
    own_c = pltpu.make_async_copy(cw, c_out.at[c, y], osem.at[1])
    own_c.start()

    arrived(g_ly)
    lq[...] = ls[y] + total([ly[i] for i in range(NY - 1)])
    g_lz = [send(lq.at[zs[i]], lz.at[i], to_z[i]) for i in range(NZ - 1)]
    arrived(g_r)
    rsum[...] = rt[x] + (rf[0] + rf[1])
    own_r.start()
    arrived(g_lz)
    lw[...] = lq[z] + total([lz[i] for i in range(NZ - 1)])
    own_l = pltpu.make_async_copy(lw, l_out, osem.at[2])
    own_l.start()

    own_r.wait()
    own_c.wait()
    arrived(g_ag)
    own_l.wait()
    for copy in sent:
        copy.wait_send()


def rows_of(a, t):
    return jnp.broadcast_to(a[t : t + 1, :], (8, LP))


def lanes_of(a, t):
    return jnp.broadcast_to(a[:, t : t + 1], (8, LP))


def solve_kernel(rank_l, c_ref, l_ref, r_hbm, core_ref, range_hbm, ct, rbuf, rsem, wsem):
    fetch = pltpu.make_async_copy(r_hbm, rbuf, rsem)
    fetch.start()
    pr = c_ref.shape[2]
    for k in range(2 * NY):
        ct[k * pr : (k + 1) * pr, :] = c_ref[k // NY, k % NY]
    cm = ct[...]
    gram = dot(cm, cm, ((0,), (0,)), HIGHEST)
    row = lax.broadcasted_iota(jnp.int32, (LP, LP), 0)
    col = lax.broadcasted_iota(jnp.int32, (LP, LP), 1)
    gram = gram + jnp.where(row == col, 0.5, 0.0)
    sub = lax.broadcasted_iota(jnp.int32, (8, LP), 0)
    lane = lax.broadcasted_iota(jnp.int32, (8, LP), 1)

    write = pltpu.make_async_copy(rbuf, range_hbm, wsem)
    tiles = [gram[8 * i : 8 * i + 8, :] for i in range(LP // 8)]
    rhs = l_ref[...]
    panels = rank_l // 8
    for kb in range(panels):
        base = 8 * kb
        p = tiles[kb]
        cols = [lanes_of(p, base + t) for t in range(8)]
        for t in range(8):
            ct_ = cols[t]
            inv = 1.0 / rows_of(ct_, t)
            here = lane == base + t
            prow = jnp.where(here, inv, rows_of(p, t) * inv)
            p = jnp.where(sub == t, prow, jnp.where(here, 0.0, p) - ct_ * prow)
            for j in range(t + 1, 8):
                crow = rows_of(cols[j], t) * inv
                cols[j] = jnp.where(sub == t, crow, cols[j] - ct_ * crow)
        inside = (lane >= base) & (lane < base + 8)
        w = jnp.where(inside, -p, p)
        ws = [rows_of(w, t) for t in range(8)]

        def update(a):
            terms = [lanes_of(a, base + t) * ws[t] for t in range(8)]
            while len(terms) > 1:
                terms = [terms[i] + terms[i + 1] for i in range(0, len(terms), 2)]
            return jnp.where(inside, 0.0, a) - terms[0]

        for i in range(kb + 1, panels):
            tiles[i] = update(tiles[i])
        rhs = update(rhs)
        if kb == panels // 2:
            fetch.wait()
            write.start()
    core = dot(rhs, cm, ((1,), (1,)), HIGHEST)
    core_ref[...] = core[:, 0 : core_ref.shape[1]]
    write.wait()


VMEM = pl.BlockSpec(memory_space=pltpu.VMEM)
ANY = pl.BlockSpec(memory_space=pl.ANY)


def on_device(snapshots, left_slow, left_fast, right_slow, right_fast):
    nx = lax.axis_size("samp")
    rows, samples = snapshots.shape
    rank_l, rank_r = left_slow.shape[0], right_slow.shape[0]
    part = rows // nx
    pr = -(-rank_r // (2 * NY))
    f32 = lambda *shape: jax.ShapeDtypeStruct(shape, F32)
    vm = lambda *shape: pltpu.VMEM(shape, F32)
    dma = lambda *shape: pltpu.SemaphoreType.DMA(shape)
    copies = 4 + 2 * (2 * NY - 1) + (nx - 1) + (NZ - 1) + 1 + (NY - 1) + (NZ - 1)
    small = [left_slow.T, left_fast.T, right_slow.T, right_fast.T]
    cf, lf, rf = pl.pallas_call(
        functools.partial(sketch_kernel, nx, part),
        in_specs=[ANY] * 5,
        out_specs=(ANY,) * 3,
        out_shape=(f32(2, NY, pr, LP), f32(8, LP), f32(rank_r, part)),
        scratch_shapes=[pltpu.VMEM(a.shape, BF16) for a in small] + [
            pltpu.VMEM((rows, samples), BF16),
            pltpu.VMEM((rank_l, rows), BF16),
            pltpu.VMEM((rank_r, samples), BF16),
            vm(LP, samples), vm(2 * NY * pr, LP), vm(nx, rank_r, part),
            vm(2, NY, NZ, 8, LP), vm(2, NY, pr, LP),
            vm(2 * NY - 1, pr, LP), vm(pr, LP), vm(nx - 1, pr, LP), vm(pr, LP),
            vm(NZ - 1, pr, LP), vm(pr, LP),
            vm(NY, NZ, 8, LP), vm(NY, NZ, 8, LP), vm(NY - 1, NZ, 8, LP), vm(NZ, 8, LP),
            vm(NZ - 1, 8, LP), vm(8, LP),
            vm(rank_r, part // 2), vm(rank_r, part // 2), vm(rank_r, part), vm(rank_r, part),
            vm(2, rank_r, part), vm(rank_r, part),
            dma(nx), dma(4), dma(copies), dma(copies), dma(3),
        ],
        compiler_params=pltpu.CompilerParams(collective_id=0, has_side_effects=True),
        name="sketch",
    )(snapshots, *small)

    core_t, range_t = pl.pallas_call(
        functools.partial(solve_kernel, rank_l),
        in_specs=[VMEM, VMEM, ANY],
        out_specs=(VMEM, ANY),
        out_shape=(f32(8, rank_r), f32(rank_r, part)),
        scratch_shapes=[
            vm(2 * NY * pr, LP), vm(rank_r, part),
            pltpu.SemaphoreType.DMA, pltpu.SemaphoreType.DMA,
        ],
        name="solve",
    )(cf, lf, rf)
    return (range_t.T, core_t.T)


def solution(mesh):
    placed = (P("cells", "samp"), P(None, "cells"), P(), P(None, "samp"), P())
    return jax.shard_map(
        on_device,
        mesh=mesh,
        in_specs=placed,
        out_specs=(P(("cells", "samp"), None), P(None, ("samp", "cells"))),
        check_vma=False,
    )
```

```python
import functools

import jax
import jax.numpy as jnp
from jax import lax
from jax.experimental import pallas as pl
from jax.experimental.pallas import tpu as pltpu
from jax.sharding import PartitionSpec as P

F32 = jnp.float32
BF16 = jnp.bfloat16
MESH = pl.DeviceIdType.MESH
NY, NZ = 8, 8
LP = 128
HIGHEST = lax.Precision.HIGHEST


def dot(a, b, dims, precision=None):
    return lax.dot_general(a, b, (dims, ((), ())), precision=precision, preferred_element_type=F32)


def total(terms):
    return functools.reduce(lambda a, b: a + b, terms)


def expand_rows(slow_t, fast_t, width):
    ns, nf = slow_t.shape[0], fast_t.shape[0]
    n = lax.broadcasted_iota(jnp.int32, (ns, width), 1)
    a = lax.broadcasted_iota(jnp.int32, (ns, width), 0)
    pick_slow = jnp.where(n // nf == a, 1.0, 0.0).astype(BF16)
    n = lax.broadcasted_iota(jnp.int32, (nf, width), 1)
    b = lax.broadcasted_iota(jnp.int32, (nf, width), 0)
    pick_fast = jnp.where(n % nf == b, 1.0, 0.0).astype(BF16)
    dims = ((0,), (0,))
    return (dot(slow_t, pick_slow, dims) * dot(fast_t, pick_fast, dims)).astype(BF16)


def sketch_kernel(
    nx, part,
    x_hbm, ls_hbm, lf_hbm, rs_hbm, rf_hbm,
    c_out, l_out, r_out,
    ls_ref, lf_ref, rs_ref, rf_ref, xb, psi, omega, acc, ct, rt, lt, cp,
    cy, cq, cx, cr, cz, cw,
    lc, ls, ly, lq, lz, lw,
    ra, rb, rl, rr, rf, rsum,
    xsem, wsem, ssem, rsem, osem,
):
    cell = lax.axis_index("cells")
    x = lax.axis_index("samp")
    c = lax.rem(cell, 2)
    z = lax.rem(cell // 2, NZ)
    y = cell // (2 * NZ)
    rank_l, rank_r = ls_ref.shape[1], rs_ref.shape[1]
    samples = xb.shape[1]
    pr = cp.shape[2]

    def at(y_, z_, c_, x_):
        return ((y_ * NZ + z_) * 2 + c_, x_)

    ys = [lax.rem(y + d, NY) for d in range(1, NY)]
    zs = [lax.rem(z + d, NZ) for d in range(1, NZ)]
    xs = [lax.rem(x + d, nx) for d in range(1, nx)]
    other = at(y, z, 1 - c, x)
    to_y = [at(p, z, c, x) for p in ys]
    to_yc = [at(p, z, 1 - c, x) for p in ys]
    to_z = [at(y, p, c, x) for p in zs]
    to_x = [at(y, z, c, p) for p in xs]
    right, left = to_x[0], to_x[-1]

    barrier = pltpu.get_barrier_semaphore()
    peers = [other] + to_y + to_yc + to_z + to_x
    for peer in peers:
        pl.semaphore_signal(barrier, inc=1, device_id=peer, device_id_type=MESH)

    small = [
        pltpu.make_async_copy(src, dst, wsem.at[i])
        for i, (src, dst) in enumerate(
            [(ls_hbm, ls_ref), (lf_hbm, lf_ref), (rs_hbm, rs_ref), (rf_hbm, rf_ref)]
        )
    ]
    loads = []
    for i in range(nx):
        span = pl.ds(i * part, part)
        loads.append(pltpu.make_async_copy(x_hbm.at[span], xb.at[span], xsem.at[i]))
    for copy in small + loads:
        copy.start()

    used = [0]
    sent = []

    def remote(src, dst, peer):
        k = used[0]
        used[0] += 1
        copy = pltpu.make_async_remote_copy(
            src_ref=src, dst_ref=dst, send_sem=ssem.at[k], recv_sem=rsem.at[k],
            device_id=peer, device_id_type=MESH,
        )
        sent.append(copy)
        return copy

    def send(src, dst, peer):
        copy = remote(src, dst, peer)
        copy.start()
        return copy

    def arrived(copies):
        for copy in copies:
            copy.wait_recv()

    early = z < NZ // 2
    late = jnp.logical_not(early)
    half = part // 2
    lo, hi = pl.ds(0, half), pl.ds(half, half)
    far = lax.rem(x + 2, nx)
    xr, xl = xs[0], xs[-1]
    g_ra = [remote(rt.at[far, :, lo], ra, right), remote(rt.at[far, :, hi], rb, left)]
    g_r = [remote(rl, rf.at[0], right), remote(rr, rf.at[1], left)]
    own_r = pltpu.make_async_copy(rsum, r_out, osem.at[0])

    def range_product():
        for i in range(nx):
            rt[i] = dot(omega[...], xb[i * part : (i + 1) * part, :], ((1,), (1,)))

    def range_first():
        for copy in g_ra:
            copy.start()

    def range_second():
        arrived(g_ra)
        rl[:, lo] = rt[xr, :, lo] + ra[...]
        rl[:, hi] = rt[xr, :, hi]
        rr[:, lo] = rt[xl, :, lo]
        rr[:, hi] = rt[xl, :, hi] + rb[...]
        for copy in g_r:
            copy.start()

    for copy in small:
        copy.wait()
    omega[...] = expand_rows(rs_ref[...], rf_ref[...], samples)
    psi[...] = expand_rows(ls_ref[...], lf_ref[...], nx * part)
    acc[rank_l:, :] = jnp.zeros((LP - rank_l, samples), F32)
    for i in range(nx):
        loads[i].wait()
        rows = slice(i * part, (i + 1) * part)
        term = dot(psi[:, rows], xb[rows, :], ((1,), (0,)))
        acc[0:rank_l, :] = term if i == 0 else acc[0:rank_l, :] + term

    left_part = acc[0:rank_l, :]
    top = left_part.astype(BF16)
    rest = left_part - top.astype(F32)
    mid = rest.astype(BF16)
    low = (rest - mid.astype(F32)).astype(BF16)
    om = omega[...]
    dims = ((1,), (1,))
    ct[...] = jnp.zeros_like(ct)
    ct[0:rank_r, 0:rank_l] = dot(om, top, dims) + (dot(om, mid, dims) + dot(om, low, dims))
    for k in range(2 * NY):
        cp[k // NY, k % NY] = ct[k * pr : (k + 1) * pr, :]

    @pl.when(early)
    def _():
        range_product()

    pl.semaphore_wait(barrier, len(peers))

    g_cy = [send(cp.at[c, ys[i]], cy.at[i], to_y[i]) for i in range(NY - 1)]
    g_cy += [send(cp.at[1 - c, ys[i]], cy.at[NY - 1 + i], to_yc[i]) for i in range(NY - 1)]
    g_cy += [send(cp.at[1 - c, y], cy.at[2 * NY - 2], other)]

    @pl.when(early)
    def _():
        range_first()

    left_t = acc[...].T
    for j in range(samples // 8):
        lt[j % 2, j // (2 * NZ), (j // 2) % NZ] = left_t[8 * j : 8 * j + 8, :]
    g_lc = [send(lt.at[1 - c], lc, other)]

    @pl.when(late)
    def _():
        range_product()

    arrived(g_lc)
    ls[...] = lt[c] + lc[...]

    arrived(g_cy)
    cq[...] = cp[c, y] + total([cy[i] for i in range(2 * NY - 1)])
    g_cx = [send(cq, cx.at[i], to_x[i]) for i in range(nx - 1)]

    @pl.when(early)
    def _():
        range_second()

    @pl.when(late)
    def _():
        range_first()

    g_ly = [send(ls.at[ys[i]], ly.at[i], to_y[i]) for i in range(NY - 1)]

    arrived(g_cx)
    cr[...] = cq[...] + total([cx[i] for i in range(nx - 1)])
    g_cz = [send(cr, cz.at[i], to_z[i]) for i in range(NZ - 1)]

    @pl.when(late)
    def _():
        range_second()

    arrived(g_cz)
    cw[...] = cr[...] + total([cz[i] for i in range(NZ - 1)])
    g_ag = [send(cw, c_out.at[c, y], to_y[i]) for i in range(NY - 1)]
    g_ag += [send(cw, c_out.at[c, y], to_yc[i]) for i in range(NY - 1)]
    g_ag += [send(cw, c_out.at[c, y], other)]
    own_c = pltpu.make_async_copy(cw, c_out.at[c, y], osem.at[1])
    own_c.start()

    arrived(g_ly)
    lq[...] = ls[y] + total([ly[i] for i in range(NY - 1)])
    g_lz = [send(lq.at[zs[i]], lz.at[i], to_z[i]) for i in range(NZ - 1)]
    arrived(g_r)
    rsum[...] = rt[x] + (rf[0] + rf[1])
    own_r.start()
    arrived(g_lz)
    lw[...] = lq[z] + total([lz[i] for i in range(NZ - 1)])
    own_l = pltpu.make_async_copy(lw, l_out, osem.at[2])
    own_l.start()

    own_r.wait()
    own_c.wait()
    arrived(g_ag)
    own_l.wait()
    for copy in sent:
        copy.wait_send()


def rows_of(a, t):
    return jnp.broadcast_to(a[t : t + 1, :], (8, LP))


def lanes_of(a, t):
    return jnp.broadcast_to(a[:, t : t + 1], (8, LP))


def solve_kernel(rank_l, c_ref, l_ref, r_hbm, core_ref, range_hbm, ct, rbuf, rsem, wsem):
    fetch = pltpu.make_async_copy(r_hbm, rbuf, rsem)
    fetch.start()
    pr = c_ref.shape[2]
    for k in range(2 * NY):
        ct[k * pr : (k + 1) * pr, :] = c_ref[k // NY, k % NY]
    cm = ct[...]
    gram = dot(cm, cm, ((0,), (0,)), HIGHEST)
    row = lax.broadcasted_iota(jnp.int32, (LP, LP), 0)
    col = lax.broadcasted_iota(jnp.int32, (LP, LP), 1)
    gram = gram + jnp.where(row == col, 0.5, 0.0)
    sub = lax.broadcasted_iota(jnp.int32, (8, LP), 0)
    lane = lax.broadcasted_iota(jnp.int32, (8, LP), 1)

    write = pltpu.make_async_copy(rbuf, range_hbm, wsem)
    tiles = [gram[8 * i : 8 * i + 8, :] for i in range(LP // 8)]
    rhs = l_ref[...]
    panels = rank_l // 8
    for kb in range(panels):
        base = 8 * kb
        p = tiles[kb]
        cols = [lanes_of(p, base + t) for t in range(8)]
        for t in range(8):
            ct_ = cols[t]
            inv = 1.0 / rows_of(ct_, t)
            here = lane == base + t
            prow = jnp.where(here, inv, rows_of(p, t) * inv)
            p = jnp.where(sub == t, prow, jnp.where(here, 0.0, p) - ct_ * prow)
            for j in range(t + 1, 8):
                crow = rows_of(cols[j], t) * inv
                cols[j] = jnp.where(sub == t, crow, cols[j] - ct_ * crow)
        inside = (lane >= base) & (lane < base + 8)
        w = jnp.where(inside, -p, p)
        ws = [rows_of(w, t) for t in range(8)]

        def update(a):
            terms = [lanes_of(a, base + t) * ws[t] for t in range(8)]
            while len(terms) > 1:
                terms = [terms[i] + terms[i + 1] for i in range(0, len(terms), 2)]
            return jnp.where(inside, 0.0, a) - terms[0]

        for i in range(kb + 1, panels):
            tiles[i] = update(tiles[i])
        rhs = update(rhs)
        if kb == panels // 2:
            fetch.wait()
            write.start()
    core = dot(rhs, cm, ((1,), (1,)), HIGHEST)
    core_ref[...] = core[:, 0 : core_ref.shape[1]]
    write.wait()


VMEM = pl.BlockSpec(memory_space=pltpu.VMEM)
ANY = pl.BlockSpec(memory_space=pl.ANY)


def on_device(snapshots, left_slow, left_fast, right_slow, right_fast):
    nx = lax.axis_size("samp")
    rows, samples = snapshots.shape
    rank_l, rank_r = left_slow.shape[0], right_slow.shape[0]
    part = rows // nx
    pr = -(-rank_r // (2 * NY))
    f32 = lambda *shape: jax.ShapeDtypeStruct(shape, F32)
    vm = lambda *shape: pltpu.VMEM(shape, F32)
    dma = lambda *shape: pltpu.SemaphoreType.DMA(shape)
    copies = 4 + 2 * (2 * NY - 1) + (nx - 1) + (NZ - 1) + 1 + (NY - 1) + (NZ - 1)
    small = [left_slow.T, left_fast.T, right_slow.T, right_fast.T]
    cf, lf, rf = pl.pallas_call(
        functools.partial(sketch_kernel, nx, part),
        in_specs=[ANY] * 5,
        out_specs=(ANY,) * 3,
        out_shape=(f32(2, NY, pr, LP), f32(8, LP), f32(rank_r, part)),
        scratch_shapes=[pltpu.VMEM(a.shape, BF16) for a in small] + [
            pltpu.VMEM((rows, samples), BF16),
            pltpu.VMEM((rank_l, rows), BF16),
            pltpu.VMEM((rank_r, samples), BF16),
            vm(LP, samples), vm(2 * NY * pr, LP), vm(nx, rank_r, part),
            vm(2, NY, NZ, 8, LP), vm(2, NY, pr, LP),
            vm(2 * NY - 1, pr, LP), vm(pr, LP), vm(nx - 1, pr, LP), vm(pr, LP),
            vm(NZ - 1, pr, LP), vm(pr, LP),
            vm(NY, NZ, 8, LP), vm(NY, NZ, 8, LP), vm(NY - 1, NZ, 8, LP), vm(NZ, 8, LP),
            vm(NZ - 1, 8, LP), vm(8, LP),
            vm(rank_r, part // 2), vm(rank_r, part // 2), vm(rank_r, part), vm(rank_r, part),
            vm(2, rank_r, part), vm(rank_r, part),
            dma(nx), dma(4), dma(copies), dma(copies), dma(3),
        ],
        compiler_params=pltpu.CompilerParams(
            collective_id=0, has_side_effects=True, vmem_limit_bytes=24 << 20
        ),
        name="sketch",
    )(*[pltpu.with_memory_space_constraint(a, pltpu.HBM) for a in [snapshots] + small])

    core_t, range_t = pl.pallas_call(
        functools.partial(solve_kernel, rank_l),
        in_specs=[VMEM, VMEM, ANY],
        out_specs=(VMEM, ANY),
        out_shape=(f32(8, rank_r), f32(rank_r, part)),
        scratch_shapes=[
            vm(2 * NY * pr, LP), vm(rank_r, part),
            pltpu.SemaphoreType.DMA, pltpu.SemaphoreType.DMA,
        ],
        compiler_params=pltpu.CompilerParams(vmem_limit_bytes=8 << 20),
        name="solve",
    )(cf, lf, rf)
    return (range_t.T, core_t.T)


def solution(mesh):
    placed = (P("cells", "samp"), P(None, "cells"), P(), P(None, "samp"), P())
    return jax.shard_map(
        on_device,
        mesh=mesh,
        in_specs=placed,
        out_specs=(P(("cells", "samp"), None), P(None, ("samp", "cells"))),
        check_vma=False,
    )
```

```python
import functools

import jax
import jax.numpy as jnp
from jax import lax
from jax.experimental import pallas as pl
from jax.experimental.pallas import tpu as pltpu
from jax.sharding import PartitionSpec as P

F32 = jnp.float32
BF16 = jnp.bfloat16
MESH = pl.DeviceIdType.MESH
NY, NZ = 8, 8
LP = 128
HIGHEST = lax.Precision.HIGHEST


def dot(a, b, dims, precision=None):
    return lax.dot_general(a, b, (dims, ((), ())), precision=precision, preferred_element_type=F32)


def far_first(n):
    return sorted(range(n - 1), key=lambda i: -min(i + 1, n - 1 - i))


def total(terms):
    return functools.reduce(lambda a, b: a + b, terms)


def expand_rows(slow_t, fast_t, width):
    ns, nf = slow_t.shape[0], fast_t.shape[0]
    n = lax.broadcasted_iota(jnp.int32, (ns, width), 1)
    a = lax.broadcasted_iota(jnp.int32, (ns, width), 0)
    pick_slow = jnp.where(n // nf == a, 1.0, 0.0).astype(BF16)
    n = lax.broadcasted_iota(jnp.int32, (nf, width), 1)
    b = lax.broadcasted_iota(jnp.int32, (nf, width), 0)
    pick_fast = jnp.where(n % nf == b, 1.0, 0.0).astype(BF16)
    dims = ((0,), (0,))
    return (dot(slow_t, pick_slow, dims) * dot(fast_t, pick_fast, dims)).astype(BF16)


def sketch_kernel(
    nx, part,
    x_hbm, ls_hbm, lf_hbm, rs_hbm, rf_hbm,
    c_out, l_out, r_out,
    ls_ref, lf_ref, rs_ref, rf_ref, xb, psi, omega, acc, ct, rt, lt, cp,
    cy, cq, cx, cr, cz, cw,
    lc, ls, ly, lq, lz, lw,
    ra, rb, rl, rr, rf, rsum,
    xsem, wsem, ssem, rsem, osem,
):
    cell = lax.axis_index("cells")
    x = lax.axis_index("samp")
    c = lax.rem(cell, 2)
    z = lax.rem(cell // 2, NZ)
    y = cell // (2 * NZ)
    rank_l, rank_r = ls_ref.shape[1], rs_ref.shape[1]
    samples = xb.shape[1]
    pr = cp.shape[2]

    def at(y_, z_, c_, x_):
        return ((y_ * NZ + z_) * 2 + c_, x_)

    ys = [lax.rem(y + d, NY) for d in range(1, NY)]
    zs = [lax.rem(z + d, NZ) for d in range(1, NZ)]
    xs = [lax.rem(x + d, nx) for d in range(1, nx)]
    other = at(y, z, 1 - c, x)
    to_y = [at(p, z, c, x) for p in ys]
    to_yc = [at(p, z, 1 - c, x) for p in ys]
    to_z = [at(y, p, c, x) for p in zs]
    to_x = [at(y, z, c, p) for p in xs]
    right, left = to_x[0], to_x[-1]

    barrier = pltpu.get_barrier_semaphore()
    peers = [other] + to_y + to_yc + to_z + to_x
    for peer in peers:
        pl.semaphore_signal(barrier, inc=1, device_id=peer, device_id_type=MESH)

    small = [
        pltpu.make_async_copy(src, dst, wsem.at[i])
        for i, (src, dst) in enumerate(
            [(ls_hbm, ls_ref), (lf_hbm, lf_ref), (rs_hbm, rs_ref), (rf_hbm, rf_ref)]
        )
    ]
    loads = []
    for i in range(nx):
        span = pl.ds(i * part, part)
        loads.append(pltpu.make_async_copy(x_hbm.at[span], xb.at[span], xsem.at[i]))
    for copy in small + loads:
        copy.start()

    used = [0]
    sent = []

    def remote(src, dst, peer):
        k = used[0]
        used[0] += 1
        copy = pltpu.make_async_remote_copy(
            src_ref=src, dst_ref=dst, send_sem=ssem.at[k], recv_sem=rsem.at[k],
            device_id=peer, device_id_type=MESH,
        )
        sent.append(copy)
        return copy

    def send(src, dst, peer):
        copy = remote(src, dst, peer)
        copy.start()
        return copy

    def arrived(copies):
        for copy in copies:
            copy.wait_recv()

    early = z < NZ // 2
    late = jnp.logical_not(early)
    half = part // 2
    lo, hi = pl.ds(0, half), pl.ds(half, half)
    far = lax.rem(x + 2, nx)
    xr, xl = xs[0], xs[-1]
    g_ra = [remote(rt.at[far, :, lo], ra, right), remote(rt.at[far, :, hi], rb, left)]
    g_r = [remote(rl, rf.at[0], right), remote(rr, rf.at[1], left)]
    own_r = pltpu.make_async_copy(rsum, r_out, osem.at[0])

    def range_product():
        for i in range(nx):
            rt[i] = dot(omega[...], xb[i * part : (i + 1) * part, :], ((1,), (1,)))

    def range_first():
        for copy in g_ra:
            copy.start()

    def range_second():
        arrived(g_ra)
        rl[:, lo] = rt[xr, :, lo] + ra[...]
        rl[:, hi] = rt[xr, :, hi]
        rr[:, lo] = rt[xl, :, lo]
        rr[:, hi] = rt[xl, :, hi] + rb[...]
        for copy in g_r:
            copy.start()

    for copy in small:
        copy.wait()
    omega[...] = expand_rows(rs_ref[...], rf_ref[...], samples)
    psi[...] = expand_rows(ls_ref[...], lf_ref[...], nx * part)
    acc[rank_l:, :] = jnp.zeros((LP - rank_l, samples), F32)
    for i in range(nx):
        loads[i].wait()
        rows = slice(i * part, (i + 1) * part)
        term = dot(psi[:, rows], xb[rows, :], ((1,), (0,)))
        acc[0:rank_l, :] = term if i == 0 else acc[0:rank_l, :] + term

    left_part = acc[0:rank_l, :]
    top = left_part.astype(BF16)
    rest = left_part - top.astype(F32)
    mid = rest.astype(BF16)
    low = (rest - mid.astype(F32)).astype(BF16)
    om = omega[...]
    dims = ((1,), (1,))
    ct[...] = jnp.zeros_like(ct)
    ct[0:rank_r, 0:rank_l] = dot(om, top, dims) + (dot(om, mid, dims) + dot(om, low, dims))
    for k in range(2 * NY):
        cp[k // NY, k % NY] = ct[k * pr : (k + 1) * pr, :]

    @pl.when(early)
    def _():
        range_product()

    pl.semaphore_wait(barrier, len(peers))

    g_cy = []
    for i in far_first(NY):
        g_cy.append(send(cp.at[c, ys[i]], cy.at[i], to_y[i]))
        g_cy.append(send(cp.at[1 - c, ys[i]], cy.at[NY - 1 + i], to_yc[i]))
    g_cy.append(send(cp.at[1 - c, y], cy.at[2 * NY - 2], other))

    @pl.when(early)
    def _():
        range_first()

    left_t = acc[...].T
    for j in range(samples // 8):
        lt[j % 2, j // (2 * NZ), (j // 2) % NZ] = left_t[8 * j : 8 * j + 8, :]
    g_lc = [send(lt.at[1 - c], lc, other)]

    @pl.when(late)
    def _():
        range_product()

    arrived(g_lc)
    ls[...] = lt[c] + lc[...]

    arrived(g_cy)
    cq[...] = cp[c, y] + total([cy[i] for i in range(2 * NY - 1)])
    g_cx = [send(cq, cx.at[i], to_x[i]) for i in far_first(nx)]

    @pl.when(early)
    def _():
        range_second()

    @pl.when(late)
    def _():
        range_first()

    g_ly = [send(ls.at[ys[i]], ly.at[i], to_y[i]) for i in range(NY - 1)]

    arrived(g_cx)
    cr[...] = cq[...] + total([cx[i] for i in range(nx - 1)])
    g_cz = [send(cr, cz.at[i], to_z[i]) for i in far_first(NZ)]

    @pl.when(late)
    def _():
        range_second()

    arrived(g_cz)
    cw[...] = cr[...] + total([cz[i] for i in range(NZ - 1)])
    g_ag = []
    for i in far_first(NY):
        g_ag += [send(cw, c_out.at[c, y], peer) for peer in (to_y[i], to_yc[i])]
    g_ag.append(send(cw, c_out.at[c, y], other))
    own_c = pltpu.make_async_copy(cw, c_out.at[c, y], osem.at[1])
    own_c.start()

    arrived(g_ly)
    lq[...] = ls[y] + total([ly[i] for i in range(NY - 1)])
    g_lz = [send(lq.at[zs[i]], lz.at[i], to_z[i]) for i in range(NZ - 1)]
    arrived(g_r)
    rsum[...] = rt[x] + (rf[0] + rf[1])
    own_r.start()
    arrived(g_lz)
    lw[...] = lq[z] + total([lz[i] for i in range(NZ - 1)])
    own_l = pltpu.make_async_copy(lw, l_out, osem.at[2])
    own_l.start()

    own_r.wait()
    own_c.wait()
    arrived(g_ag)
    own_l.wait()
    for copy in sent:
        copy.wait_send()


def rows_of(a, t):
    return jnp.broadcast_to(a[t : t + 1, :], (8, LP))


def lanes_of(a, t):
    return jnp.broadcast_to(a[:, t : t + 1], (8, LP))


def solve_kernel(rank_l, c_ref, l_ref, r_hbm, core_ref, range_hbm, ct, wsem, fence):
    write = pltpu.make_async_copy(r_hbm, range_hbm, wsem)
    write.start()
    pr = c_ref.shape[2]
    for k in range(2 * NY):
        ct[k * pr : (k + 1) * pr, :] = c_ref[k // NY, k % NY]
    cm = ct[...]
    gram = dot(cm, cm, ((0,), (0,)), HIGHEST)
    row = lax.broadcasted_iota(jnp.int32, (LP, LP), 0)
    col = lax.broadcasted_iota(jnp.int32, (LP, LP), 1)
    gram = gram + jnp.where(row == col, 0.5, 0.0)
    sub = lax.broadcasted_iota(jnp.int32, (8, LP), 0)
    lane = lax.broadcasted_iota(jnp.int32, (8, LP), 1)

    tiles = [gram[8 * i : 8 * i + 8, :] for i in range(rank_l // 8)] + [l_ref[...]]
    panels = rank_l // 8
    for kb in range(panels):
        base = 8 * kb
        p = tiles[kb]
        cols = [lanes_of(p, base + t) for t in range(8)]
        for t in range(8):
            ct_ = cols[t]
            inv = 1.0 / rows_of(ct_, t)
            here = lane == base + t
            prow = jnp.where(here, inv, rows_of(p, t) * inv)
            p = jnp.where(sub == t, prow, jnp.where(here, 0.0, p) - ct_ * prow)
            for j in range(t + 1, 8):
                crow = rows_of(cols[j], t) * inv
                cols[j] = jnp.where(sub == t, crow, cols[j] - ct_ * crow)
        inside = (lane >= base) & (lane < base + 8)
        w = jnp.where(inside, -p, p)
        ws = [rows_of(w, t) for t in range(8)]

        olds = tiles[kb + 1 :]
        news = [jnp.where(inside, 0.0, a) for a in olds]
        for group in ([0], range(1, len(olds))):
            for t in range(8):
                for i in group:
                    news[i] = news[i] - lanes_of(olds[i], base + t) * ws[t]
        tiles[kb + 1 :] = news
        pl.semaphore_signal(fence, 1)
        pl.semaphore_wait(fence, 1)
    rhs = tiles[panels]
    core = dot(rhs, cm, ((1,), (1,)), HIGHEST)
    core_ref[...] = core[:, 0 : core_ref.shape[1]]
    write.wait()


VMEM = pl.BlockSpec(memory_space=pltpu.VMEM)
ANY = pl.BlockSpec(memory_space=pl.ANY)


def on_device(snapshots, left_slow, left_fast, right_slow, right_fast):
    nx = lax.axis_size("samp")
    rows, samples = snapshots.shape
    rank_l, rank_r = left_slow.shape[0], right_slow.shape[0]
    part = rows // nx
    pr = -(-rank_r // (2 * NY))
    f32 = lambda *shape: jax.ShapeDtypeStruct(shape, F32)
    vm = lambda *shape: pltpu.VMEM(shape, F32)
    dma = lambda *shape: pltpu.SemaphoreType.DMA(shape)
    copies = 4 + 2 * (2 * NY - 1) + (nx - 1) + (NZ - 1) + 1 + (NY - 1) + (NZ - 1)
    small = [left_slow.T, left_fast.T, right_slow.T, right_fast.T]
    cf, lf, rf = pl.pallas_call(
        functools.partial(sketch_kernel, nx, part),
        in_specs=[ANY] * 5,
        out_specs=(ANY,) * 3,
        out_shape=(f32(2, NY, pr, LP), f32(8, LP), f32(rank_r, part)),
        scratch_shapes=[pltpu.VMEM(a.shape, BF16) for a in small] + [
            pltpu.VMEM((rows, samples), BF16),
            pltpu.VMEM((rank_l, rows), BF16),
            pltpu.VMEM((rank_r, samples), BF16),
            vm(LP, samples), vm(2 * NY * pr, LP), vm(nx, rank_r, part),
            vm(2, NY, NZ, 8, LP), vm(2, NY, pr, LP),
            vm(2 * NY - 1, pr, LP), vm(pr, LP), vm(nx - 1, pr, LP), vm(pr, LP),
            vm(NZ - 1, pr, LP), vm(pr, LP),
            vm(NY, NZ, 8, LP), vm(NY, NZ, 8, LP), vm(NY - 1, NZ, 8, LP), vm(NZ, 8, LP),
            vm(NZ - 1, 8, LP), vm(8, LP),
            vm(rank_r, part // 2), vm(rank_r, part // 2), vm(rank_r, part), vm(rank_r, part),
            vm(2, rank_r, part), vm(rank_r, part),
            dma(nx), dma(4), dma(copies), dma(copies), dma(3),
        ],
        compiler_params=pltpu.CompilerParams(
            collective_id=0, has_side_effects=True, vmem_limit_bytes=24 << 20
        ),
        name="sketch",
    )(*[pltpu.with_memory_space_constraint(a, pltpu.HBM) for a in [snapshots] + small])

    core_t, range_t = pl.pallas_call(
        functools.partial(solve_kernel, rank_l),
        in_specs=[VMEM, VMEM, ANY],
        out_specs=(VMEM, ANY),
        out_shape=(f32(8, rank_r), f32(rank_r, part)),
        scratch_shapes=[
            vm(2 * NY * pr, LP), pltpu.SemaphoreType.DMA, pltpu.SemaphoreType.REGULAR,
        ],
        compiler_params=pltpu.CompilerParams(vmem_limit_bytes=8 << 20),
        name="solve",
    )(cf, lf, rf)
    return (range_t.T, core_t.T)


def solution(mesh):
    placed = (P("cells", "samp"), P(None, "cells"), P(), P(None, "samp"), P())
    return jax.shard_map(
        on_device,
        mesh=mesh,
        in_specs=placed,
        out_specs=(P(("cells", "samp"), None), P(None, ("samp", "cells"))),
        check_vma=False,
    )
```

```python
import functools

import jax
import jax.numpy as jnp
from jax import lax
from jax.experimental import pallas as pl
from jax.experimental.pallas import tpu as pltpu
from jax.sharding import PartitionSpec as P

F32 = jnp.float32
BF16 = jnp.bfloat16
MESH = pl.DeviceIdType.MESH
NY, NZ = 8, 8
LP = 128
HIGHEST = lax.Precision.HIGHEST


def dot(a, b, dims, precision=None):
    return lax.dot_general(a, b, (dims, ((), ())), precision=precision, preferred_element_type=F32)


def far_first(n):
    return sorted(range(n - 1), key=lambda i: -min(i + 1, n - 1 - i))


def total(terms):
    return functools.reduce(lambda a, b: a + b, terms)


def expand_rows(slow_t, fast_t, width):
    ns, nf = slow_t.shape[0], fast_t.shape[0]
    n = lax.broadcasted_iota(jnp.int32, (ns, width), 1)
    a = lax.broadcasted_iota(jnp.int32, (ns, width), 0)
    pick_slow = jnp.where(n // nf == a, 1.0, 0.0).astype(BF16)
    n = lax.broadcasted_iota(jnp.int32, (nf, width), 1)
    b = lax.broadcasted_iota(jnp.int32, (nf, width), 0)
    pick_fast = jnp.where(n % nf == b, 1.0, 0.0).astype(BF16)
    dims = ((0,), (0,))
    return (dot(slow_t, pick_slow, dims) * dot(fast_t, pick_fast, dims)).astype(BF16)


def sketch_kernel(
    nx, part,
    x_hbm, ls_hbm, lf_hbm, rs_hbm, rf_hbm,
    c_out, l_out, r_out,
    ls_ref, lf_ref, rs_ref, rf_ref, xb, psi, omega, acc, ct, rt, lt, cp,
    cy, cq, cx, cr, cz, cw,
    lc, ls, ly, lq, lz, lw,
    ra, rb, rl, rr, rf, rsum,
    xsem, wsem, ssem, rsem, osem,
):
    cell = lax.axis_index("cells")
    x = lax.axis_index("samp")
    c = lax.rem(cell, 2)
    z = lax.rem(cell // 2, NZ)
    y = cell // (2 * NZ)
    rank_l, rank_r = ls_ref.shape[1], rs_ref.shape[1]
    samples = xb.shape[1]
    pr = cp.shape[2]

    def at(y_, z_, c_, x_):
        return ((y_ * NZ + z_) * 2 + c_, x_)

    ys = [lax.rem(y + d, NY) for d in range(1, NY)]
    zs = [lax.rem(z + d, NZ) for d in range(1, NZ)]
    xs = [lax.rem(x + d, nx) for d in range(1, nx)]
    other = at(y, z, 1 - c, x)
    to_y = [at(p, z, c, x) for p in ys]
    to_yc = [at(p, z, 1 - c, x) for p in ys]
    to_z = [at(y, p, c, x) for p in zs]
    to_x = [at(y, z, c, p) for p in xs]
    right, left = to_x[0], to_x[-1]

    barrier = pltpu.get_barrier_semaphore()
    peers = [other] + to_y + to_yc + to_z + to_x
    for peer in peers:
        pl.semaphore_signal(barrier, inc=1, device_id=peer, device_id_type=MESH)

    small = [
        pltpu.make_async_copy(src, dst, wsem.at[i])
        for i, (src, dst) in enumerate(
            [(ls_hbm, ls_ref), (lf_hbm, lf_ref), (rs_hbm, rs_ref), (rf_hbm, rf_ref)]
        )
    ]
    loads = []
    for i in range(nx):
        span = pl.ds(i * part, part)
        loads.append(pltpu.make_async_copy(x_hbm.at[span], xb.at[span], xsem.at[i]))
    for copy in small + loads:
        copy.start()

    used = [0]
    sent = []

    def remote(src, dst, peer):
        k = used[0]
        used[0] += 1
        copy = pltpu.make_async_remote_copy(
            src_ref=src, dst_ref=dst, send_sem=ssem.at[k], recv_sem=rsem.at[k],
            device_id=peer, device_id_type=MESH,
        )
        sent.append(copy)
        return copy

    def send(src, dst, peer):
        copy = remote(src, dst, peer)
        copy.start()
        return copy

    def arrived(copies):
        for copy in copies:
            copy.wait_recv()

    early = z < NZ // 2
    late = jnp.logical_not(early)
    half = part // 2
    lo, hi = pl.ds(0, half), pl.ds(half, half)
    far = lax.rem(x + 2, nx)
    xr, xl = xs[0], xs[-1]
    g_ra = [remote(rt.at[far, :, lo], ra, right), remote(rt.at[far, :, hi], rb, left)]
    g_r = [remote(rl, rf.at[0], right), remote(rr, rf.at[1], left)]
    own_r = pltpu.make_async_copy(rsum, r_out, osem.at[0])

    def range_product():
        for i in range(nx):
            rt[i] = dot(omega[...], xb[i * part : (i + 1) * part, :], ((1,), (1,)))

    def range_first():
        for copy in g_ra:
            copy.start()

    def range_second():
        arrived(g_ra)
        rl[:, lo] = rt[xr, :, lo] + ra[...]
        rl[:, hi] = rt[xr, :, hi]
        rr[:, lo] = rt[xl, :, lo]
        rr[:, hi] = rt[xl, :, hi] + rb[...]
        for copy in g_r:
            copy.start()

    for copy in small:
        copy.wait()
    omega[...] = expand_rows(rs_ref[...], rf_ref[...], samples)
    psi[...] = expand_rows(ls_ref[...], lf_ref[...], nx * part)
    acc[rank_l:, :] = jnp.zeros((LP - rank_l, samples), F32)
    for i in range(nx):
        loads[i].wait()
        rows = slice(i * part, (i + 1) * part)
        term = dot(psi[:, rows], xb[rows, :], ((1,), (0,)))
        acc[0:rank_l, :] = term if i == 0 else acc[0:rank_l, :] + term

    left_part = acc[...]
    top = left_part.astype(BF16)
    rest = left_part - top.astype(F32)
    mid = rest.astype(BF16)
    low = (rest - mid.astype(F32)).astype(BF16)
    terms = dot(omega[...], jnp.concatenate([top, mid, low], axis=0), ((1,), (1,)))
    ct[rank_r:, :] = jnp.zeros((ct.shape[0] - rank_r, LP), F32)
    ct[0:rank_r, :] = terms[:, 0:LP] + (terms[:, LP : 2 * LP] + terms[:, 2 * LP :])
    for k in range(2 * NY):
        cp[k // NY, k % NY] = ct[k * pr : (k + 1) * pr, :]

    @pl.when(early)
    def _():
        range_product()

    pl.semaphore_wait(barrier, len(peers))

    g_cy = []
    for i in far_first(NY):
        g_cy.append(send(cp.at[c, ys[i]], cy.at[i], to_y[i]))
        g_cy.append(send(cp.at[1 - c, ys[i]], cy.at[NY - 1 + i], to_yc[i]))
    g_cy.append(send(cp.at[1 - c, y], cy.at[2 * NY - 2], other))

    @pl.when(early)
    def _():
        range_first()

    left_t = acc[...].T
    for j in range(samples // 8):
        lt[j % 2, j // (2 * NZ), (j // 2) % NZ] = left_t[8 * j : 8 * j + 8, :]
    g_lc = [send(lt.at[1 - c], lc, other)]

    @pl.when(late)
    def _():
        range_product()

    arrived(g_lc)
    ls[...] = lt[c] + lc[...]

    arrived(g_cy)
    cq[...] = cp[c, y] + total([cy[i] for i in range(2 * NY - 1)])
    g_cx = [send(cq, cx.at[i], to_x[i]) for i in far_first(nx)]

    @pl.when(early)
    def _():
        range_second()

    @pl.when(late)
    def _():
        range_first()

    g_ly = [send(ls.at[ys[i]], ly.at[i], to_y[i]) for i in range(NY - 1)]

    arrived(g_cx)
    cr[...] = cq[...] + total([cx[i] for i in range(nx - 1)])
    g_cz = [send(cr, cz.at[i], to_z[i]) for i in far_first(NZ)]

    @pl.when(late)
    def _():
        range_second()

    arrived(g_cz)
    cw[...] = cr[...] + total([cz[i] for i in range(NZ - 1)])
    g_ag = []
    for i in far_first(NY):
        g_ag += [send(cw, c_out.at[c, y], peer) for peer in (to_y[i], to_yc[i])]
    g_ag.append(send(cw, c_out.at[c, y], other))
    own_c = pltpu.make_async_copy(cw, c_out.at[c, y], osem.at[1])
    own_c.start()

    arrived(g_ly)
    lq[...] = ls[y] + total([ly[i] for i in range(NY - 1)])
    g_lz = [send(lq.at[zs[i]], lz.at[i], to_z[i]) for i in range(NZ - 1)]
    arrived(g_r)
    rsum[...] = rt[x] + (rf[0] + rf[1])
    own_r.start()
    arrived(g_lz)
    lw[...] = lq[z] + total([lz[i] for i in range(NZ - 1)])
    own_l = pltpu.make_async_copy(lw, l_out, osem.at[2])
    own_l.start()

    own_r.wait()
    own_c.wait()
    arrived(g_ag)
    own_l.wait()
    for copy in sent:
        copy.wait_send()


def rows_of(a, t):
    return jnp.broadcast_to(a[t : t + 1, :], (8, LP))


def lanes_of(a, t):
    return jnp.broadcast_to(a[:, t : t + 1], (8, LP))


def solve_kernel(rank_l, c_ref, l_ref, r_hbm, core_ref, range_hbm, ct, wsem, fence):
    write = pltpu.make_async_copy(r_hbm, range_hbm, wsem)
    write.start()
    pr = c_ref.shape[2]
    for k in range(2 * NY):
        ct[k * pr : (k + 1) * pr, :] = c_ref[k // NY, k % NY]
    cm = ct[...]
    gram = dot(cm, cm, ((0,), (0,)), HIGHEST)
    row = lax.broadcasted_iota(jnp.int32, (LP, LP), 0)
    col = lax.broadcasted_iota(jnp.int32, (LP, LP), 1)
    gram = gram + jnp.where(row == col, 0.5, 0.0)
    sub = lax.broadcasted_iota(jnp.int32, (8, LP), 0)
    lane = lax.broadcasted_iota(jnp.int32, (8, LP), 1)

    tiles = [gram[8 * i : 8 * i + 8, :] for i in range(rank_l // 8)] + [l_ref[...]]
    panels = rank_l // 8
    for kb in range(panels):
        base = 8 * kb
        p = tiles[kb]
        cols = [lanes_of(p, base + t) for t in range(8)]
        for t in range(8):
            ct_ = cols[t]
            inv = 1.0 / rows_of(ct_, t)
            here = lane == base + t
            prow = jnp.where(here, inv, rows_of(p, t) * inv)
            p = jnp.where(sub == t, prow, jnp.where(here, 0.0, p) - ct_ * prow)
            for j in range(t + 1, 8):
                crow = rows_of(cols[j], t) * inv
                cols[j] = jnp.where(sub == t, crow, cols[j] - ct_ * crow)
        inside = (lane >= base) & (lane < base + 8)
        w = jnp.where(inside, -p, p)
        ws = [rows_of(w, t) for t in range(8)]

        olds = tiles[kb + 1 :]
        news = [jnp.where(inside, 0.0, a) for a in olds]
        for group in ([0], range(1, len(olds))):
            for t in range(8):
                for i in group:
                    news[i] = news[i] - lanes_of(olds[i], base + t) * ws[t]
        tiles[kb + 1 :] = news
        pl.semaphore_signal(fence, 1)
        pl.semaphore_wait(fence, 1)
    rhs = tiles[panels]
    core = dot(rhs, cm, ((1,), (1,)), HIGHEST)
    core_ref[...] = core[:, 0 : core_ref.shape[1]]
    write.wait()


VMEM = pl.BlockSpec(memory_space=pltpu.VMEM)
ANY = pl.BlockSpec(memory_space=pl.ANY)


def on_device(snapshots, left_slow, left_fast, right_slow, right_fast):
    nx = lax.axis_size("samp")
    rows, samples = snapshots.shape
    rank_l, rank_r = left_slow.shape[0], right_slow.shape[0]
    part = rows // nx
    pr = -(-rank_r // (2 * NY))
    f32 = lambda *shape: jax.ShapeDtypeStruct(shape, F32)
    vm = lambda *shape: pltpu.VMEM(shape, F32)
    dma = lambda *shape: pltpu.SemaphoreType.DMA(shape)
    copies = 4 + 2 * (2 * NY - 1) + (nx - 1) + (NZ - 1) + 1 + (NY - 1) + (NZ - 1)
    small = [left_slow.T, left_fast.T, right_slow.T, right_fast.T]
    cf, lf, rf = pl.pallas_call(
        functools.partial(sketch_kernel, nx, part),
        in_specs=[ANY] * 5,
        out_specs=(ANY,) * 3,
        out_shape=(f32(2, NY, pr, LP), f32(8, LP), f32(rank_r, part)),
        scratch_shapes=[pltpu.VMEM(a.shape, BF16) for a in small] + [
            pltpu.VMEM((rows, samples), BF16),
            pltpu.VMEM((rank_l, rows), BF16),
            pltpu.VMEM((rank_r, samples), BF16),
            vm(LP, samples), vm(2 * NY * pr, LP), vm(nx, rank_r, part),
            vm(2, NY, NZ, 8, LP), vm(2, NY, pr, LP),
            vm(2 * NY - 1, pr, LP), vm(pr, LP), vm(nx - 1, pr, LP), vm(pr, LP),
            vm(NZ - 1, pr, LP), vm(pr, LP),
            vm(NY, NZ, 8, LP), vm(NY, NZ, 8, LP), vm(NY - 1, NZ, 8, LP), vm(NZ, 8, LP),
            vm(NZ - 1, 8, LP), vm(8, LP),
            vm(rank_r, part // 2), vm(rank_r, part // 2), vm(rank_r, part), vm(rank_r, part),
            vm(2, rank_r, part), vm(rank_r, part),
            dma(nx), dma(4), dma(copies), dma(copies), dma(3),
        ],
        compiler_params=pltpu.CompilerParams(
            collective_id=0, has_side_effects=True, vmem_limit_bytes=24 << 20
        ),
        name="sketch",
    )(*[pltpu.with_memory_space_constraint(a, pltpu.HBM) for a in [snapshots] + small])

    core_t, range_t = pl.pallas_call(
        functools.partial(solve_kernel, rank_l),
        in_specs=[VMEM, VMEM, ANY],
        out_specs=(VMEM, ANY),
        out_shape=(f32(8, rank_r), f32(rank_r, part)),
        scratch_shapes=[
            vm(2 * NY * pr, LP), pltpu.SemaphoreType.DMA, pltpu.SemaphoreType.REGULAR,
        ],
        compiler_params=pltpu.CompilerParams(vmem_limit_bytes=8 << 20),
        name="solve",
    )(cf, lf, rf)
    return (range_t.T, core_t.T)


def solution(mesh):
    placed = (P("cells", "samp"), P(None, "cells"), P(), P(None, "samp"), P())
    return jax.shard_map(
        on_device,
        mesh=mesh,
        in_specs=placed,
        out_specs=(P(("cells", "samp"), None), P(None, ("samp", "cells"))),
        check_vma=False,
    )
```
